512 devices in a mesh: slab: 64 (over y, z), angle: 8 (over x, core).
Axes of the slice: x: 4, y: 4, z: 16, core: 2. Of those that a mesh axis runs over, the one named last changes fastest.
Arguments:
- object_density: bfloat16 [2, 512, 128, 320], P(None, 'slab', 'angle'), may hold values from -6 to 6
- resampling_matrices: bfloat16 [8, 64, 128], replicated, may hold values from -0.02734375 to 0.02734375
- receiving_tile_number: int32 [8, 64, 8], replicated, may hold values from 0 to 4
- illumination_modes: bfloat16 [4, 2, 256, 256], replicated, may hold values from -3 to 3
- window_corners: int32 [8, 64, 2], P('angle', 'slab'), may hold values from 1 to 63
- observed_power: float32 [8, 64, 256, 256], P('angle', 'slab'), may hold values from 0.5 to 2
Outputs:
- vol_grad: float32 [2, 512, 128, 320], P(None, 'slab', 'angle')
- probe_grad: float32 [4, 2, 256, 256], P(None, None, 'slab')
- power_mismatch: float32 [8, 64, 256, 256], P('angle', 'slab')
- locus_derivative: float32 [8, 64, 2], P('angle', 'slab')
The draws below stay inside these ranges and needn't reach their ends.
All inputs are finite; a program needn't handle non-finite values.
Results may differ from the reference program's by a relative error of at most 0.00035.
Values sent between devices are 32-bit elements; how exact they have to be, the bound alone decides.
No kernel may reach another device: no remote copies, remote signals or barrier semaphores. Data moves between devices by JAX's collectives and lax.ppermute only.
A program may use at most 64 MiB of HBM per device.

```python
import jax
import jax.numpy as jnp
from jax import lax

BEAM_WIDTH_PIX = 256
MODES = 4
UB = 64
NUB = 5
NZ = 320
TY = 16
CX = 8
TILES_DEV = 1
NUM_VIEWS = 8
NX = 512
NY = 128
NUM_FOCI = 64
N_SLAB = 64
N_ANGLE = 8


def place_ends(values, own_key, smallest, high):
    place = [jax.random.randint(jax.random.fold_in(own_key, axis), (), 0, length) for axis, length in enumerate(values.shape)]
    longest = values.shape.index(max(values.shape))
    beside = place[:longest] + [(place[longest] + 1) % values.shape[longest]] + place[longest + 1:]
    return values.at[tuple(place)].set(smallest).at[tuple(beside)].set(high)


def steps_of(own_key, extent, pieces, smallest, top_value):
    def one(position, parts):
        heights = jax.random.uniform(jax.random.fold_in(jax.random.fold_in(own_key, 6), position), (parts,), jnp.float32, smallest / len(pieces), top_value / len(pieces))
        return jnp.repeat(jnp.exp(heights), extent[position] // parts).reshape((-1,) + (1,) * (len(extent) - position - 1))

    loudness = one(*pieces[0])
    for cut in pieces[1:]:
        loudness = loudness * one(*cut)
    return loudness


def normal_values(key, extent, spread, most, split=(), kind=jnp.bfloat16):
    loudness = steps_of(key, extent, split, -0.22, 0.18) if split else 1.0
    result = jax.random.normal(key, extent, jnp.float32) * spread * loudness
    return jnp.minimum(jnp.maximum(result, -most), most).astype(kind)


def setup_inputs(seed: int = 0) -> dict:
    keys = jax.random.split(jax.random.key(seed), 7)
    object_density = normal_values(keys[0], (2, NX, NY, NZ), 1.0, 6.0, ((1, 64), (2, 8)))
    resampling_matrices = normal_values(keys[1], (NUM_VIEWS, UB, CX * TY), (4 * NX * NY // NUB) ** -0.5, 0.02734375)
    receiving_tile_number = place_ends(jax.random.randint(keys[2], (NUM_VIEWS, N_SLAB, TILES_DEV * N_ANGLE), 0, NUB), jax.random.fold_in(keys[2], 1), 0, NUB - 1).astype(jnp.int32)
    illumination_modes = normal_values(keys[3], (MODES, 2, BEAM_WIDTH_PIX, BEAM_WIDTH_PIX), 0.5, 3.0)
    window_corners = place_ends(jax.random.randint(keys[4], (NUM_VIEWS, NUM_FOCI, 2), 1, min(UB * NUB, NZ) - BEAM_WIDTH_PIX), jax.random.fold_in(keys[4], 1), 1, (min(UB * NUB, NZ) - BEAM_WIDTH_PIX) - 1).astype(jnp.int32)
    observed_power = jnp.clip(0.5 + 1.5 * jax.random.uniform(keys[5], (NUM_VIEWS, NUM_FOCI, BEAM_WIDTH_PIX, BEAM_WIDTH_PIX), jnp.float32) ** steps_of(keys[5], (NUM_VIEWS, NUM_FOCI, BEAM_WIDTH_PIX, BEAM_WIDTH_PIX), ((0, 8), (1, 64)), -0.2, 0.2), 0.5, 2.0)
    return {"object_density": object_density, "resampling_matrices": resampling_matrices, "receiving_tile_number": receiving_tile_number, "illumination_modes": illumination_modes, "window_corners": window_corners, "observed_power": observed_power}


def spot_loss(patch, illumination_modes, recorded_diffraction):
    absorb = jnp.exp(-patch[1])
    t_real = absorb * jnp.cos(patch[0])
    t_imag = absorb * jnp.sin(patch[0])
    e_real = illumination_modes[:, 0] * t_real - illumination_modes[:, 1] * t_imag
    e_imag = illumination_modes[:, 0] * t_imag + illumination_modes[:, 1] * t_real
    field = jnp.fft.fft2(e_real + 1j * e_imag, axes=(1, 2), norm='ortho')
    inten = lax.optimization_barrier(jnp.sum(jnp.real(field) ** 2 + jnp.imag(field) ** 2, axis=0))
    resid = inten - recorded_diffraction
    return (0.5 * jnp.sum(resid * resid), resid)

def reference(object_density, resampling_matrices, receiving_tile_number, illumination_modes, window_corners, observed_power):
    highest = lax.Precision.HIGHEST
    x_tiles = NX // CX
    y_tiles = NY // TY
    tiles = object_density.astype(jnp.float32).reshape(2, x_tiles, CX, y_tiles, TY, NZ)
    tiles = tiles.transpose(1, 3, 0, 2, 4, 5).reshape(x_tiles * y_tiles, 2, CX * TY, NZ)
    kernel_f = resampling_matrices.astype(jnp.float32)

    def project(angle_id):
        summed = jax.ops.segment_sum(tiles, receiving_tile_number[angle_id].reshape(-1), num_segments=NUB)
        return jnp.einsum('uk,dckz->cduz', kernel_f[angle_id], summed, precision=highest).reshape(2, NUB * UB, NZ)
    sinogram_views = lax.map(project, jnp.arange(NUM_VIEWS, dtype=jnp.int32))
    probe_f = illumination_modes.astype(jnp.float32)

    def foci_per_view(input_arrays):
        projection_at_angle, offsets_at_angle, measured_at_angle = input_arrays

        def single_spot(carry, items):
            blank_detector, probe_gradient_total = carry
            offset, recorded_diffraction = items
            col_off = offset[0].astype(jnp.int32)
            row_off = offset[1].astype(jnp.int32)
            window = lax.dynamic_slice(projection_at_angle, (jnp.int32(0), col_off - 1, row_off - 1), (2, BEAM_WIDTH_PIX + 2, BEAM_WIDTH_PIX + 2))
            patch = window[:, 1:-1, 1:-1]
            loss, pull, resid = jax.vjp(lambda patch_in, probe_in: spot_loss(patch_in, probe_in, recorded_diffraction), patch, probe_f, has_aux=True)
            patch_grad, probe_term = pull(jnp.ones((), loss.dtype))
            current = lax.dynamic_slice(blank_detector, (jnp.int32(0), col_off, row_off), (2, BEAM_WIDTH_PIX, BEAM_WIDTH_PIX))
            blank_detector = lax.dynamic_update_slice(blank_detector, current + patch_grad, (jnp.int32(0), col_off, row_off))
            shift_col = jnp.sum(patch_grad * (window[:, 2:, 1:-1] - window[:, :-2, 1:-1])) * 0.5 / BEAM_WIDTH_PIX
            shift_row = jnp.sum(patch_grad * (window[:, 1:-1, 2:] - window[:, 1:-1, :-2])) * 0.5 / BEAM_WIDTH_PIX
            return ((blank_detector, probe_gradient_total + probe_term), (resid, jnp.stack([shift_col, shift_row])))
        start_offset = (jnp.zeros((2, NUB * UB, NZ), jnp.float32), jnp.zeros_like(probe_f))
        (blank_detector, probe_gradient_total), (residual_list, scan_shifts) = lax.scan(single_spot, start_offset, (offsets_at_angle, measured_at_angle))
        return (blank_detector, probe_gradient_total, residual_list, scan_shifts)
    sinogram_derivative, illumination_derivative_parts, power_mismatch, locus_derivative = lax.map(foci_per_view, (sinogram_views, window_corners, observed_power))
    probe_grad = lax.optimization_barrier(jnp.sum(illumination_derivative_parts, axis=0))

    def back(carry, angle_id):
        blocks = jnp.einsum('uk,cduz->dckz', kernel_f[angle_id], sinogram_derivative[angle_id].reshape(2, NUB, UB, NZ), precision=highest)
        return (carry + blocks[receiving_tile_number[angle_id].reshape(-1)], None)
    start_offset = jnp.zeros((x_tiles * y_tiles, 2, CX * TY, NZ), jnp.float32)
    tile_grad, unused = lax.scan(back, start_offset, jnp.arange(NUM_VIEWS, dtype=jnp.int32))
    vol_grad = tile_grad.reshape(x_tiles, y_tiles, 2, CX, TY, NZ).transpose(2, 0, 3, 1, 4, 5).reshape(2, NX, NY, NZ)
    return (vol_grad, probe_grad, power_mismatch, locus_derivative)
```

```python
import numpy as np

import jax
import jax.numpy as jnp
from jax import lax
from jax.sharding import Mesh
from jax.sharding import PartitionSpec as P

NY, NZ, NX, NC = 4, 16, 4, 2
NA = NX * NC
NUB, UB, SIDE, DET = 5, 64, 256, 320
QC = UB // NY
LANES = 2 * DET
SLAB = ("y", "z")
ANGLE = ("x", "core")
HIGH = lax.Precision.HIGH


def dft_tables():
    k = np.arange(SIDE)
    ph = (k[:, None] * k[None, :] % SIDE) * (2.0 * np.pi / SIDE)
    c, s = np.cos(ph) / np.sqrt(SIDE), np.sin(ph) / np.sqrt(SIDE)
    fwd = np.block([[c, -s], [s, c]])
    return fwd.astype(np.float32)


def exchange(x, axes):
    return lax.all_to_all(x, axes, split_axis=0, concat_axis=0, tiled=True)


def to_tiles(q):
    n = q.shape[0] // 8
    return q.reshape(n, 8, 5, 128).transpose(0, 2, 1, 3).reshape(n * 5, 8, 128)


def from_tiles(t):
    n = t.shape[0] // 5
    return t.reshape(n, 5, 8, 128).transpose(0, 2, 1, 3).reshape(n * 8, LANES)


def sum_over_z(tiles):
    padded = jnp.pad(tiles, ((0, 14), (0, 0), (0, 0))).reshape(NZ, 4, 8, 128)
    mine = exchange(padded, "z").sum(0)
    copies = jnp.broadcast_to(mine[None], (NZ, 4, 8, 128))
    return exchange(copies, "z").reshape(64, 8, 128)[:50]


def local(volume, matrices, tile_ids, modes, corners, power):
    y, z = lax.axis_index("y"), lax.axis_index("z")
    angle = lax.axis_index(ANGLE)
    tile = volume.reshape(2, 128, DET).transpose(1, 0, 2).reshape(128, LANES)
    kern = matrices.reshape(NA, NY, QC, 128).transpose(1, 0, 2, 3).reshape(512, 128)
    ids = lax.dynamic_index_in_dim(tile_ids, angle, 0, keepdims=False)
    ids = lax.dynamic_index_in_dim(ids.reshape(NY, NZ, NA), z, 1, keepdims=False).reshape(32)

    rays = jnp.dot(kern, tile, preferred_element_type=jnp.float32).reshape(32, QC, LANES)
    items = exchange(rays, ("y", "x", "core"))
    quarter = jnp.stack(
        [jnp.sum(jnp.where((ids == d)[:, None, None], items, 0.0), axis=0) for d in range(NUB)]
    )
    summed = sum_over_z(to_tiles(quarter.reshape(NUB * QC, LANES)))
    every = lax.all_gather(summed, "y", axis=0, tiled=False)
    det = from_tiles(every.reshape(200, 8, 128))
    det = det.reshape(NY, NUB, QC, LANES).transpose(1, 0, 2, 3).reshape(DET, LANES)

    col, row = corners[0, 0, 0], corners[0, 0, 1]
    wins = [lax.dynamic_slice(det, (col - 1, k * DET + row - 1), (SIDE + 2, SIDE + 2)) for k in range(2)]
    p0, p1 = wins[0][1:-1, 1:-1], wins[1][1:-1, 1:-1]
    absorb = jnp.exp(-p1)
    tr, ti = absorb * jnp.cos(p0), absorb * jnp.sin(p0)
    probe = modes.astype(jnp.float32)
    pr, pi = probe[:, 0], probe[:, 1]
    er, ei = pr * tr - pi * ti, pr * ti + pi * tr

    fwd = jnp.asarray(dft_tables())
    ex = jnp.concatenate([er, ei], axis=2).reshape(4 * SIDE, 2 * SIDE)
    mid = jnp.dot(ex, fwd, precision=HIGH).reshape(4, SIDE, 2, SIDE)
    mid = mid.transpose(2, 1, 0, 3).reshape(2 * SIDE, 4 * SIDE)
    far = lax.dot_general(fwd, mid, (((0,), (0,)), ((), ())), precision=HIGH)
    fr, fi = far[:SIDE].reshape(SIDE, 4, SIDE), far[SIDE:].reshape(SIDE, 4, SIDE)
    resid = jnp.sum(fr * fr + fi * fi, axis=1) - power[0, 0]
    pull = far.reshape(2, SIDE, 4, SIDE) * (2.0 * resid)[None, :, None, :]
    back = jnp.dot(fwd, pull.reshape(2 * SIDE, 4 * SIDE), precision=HIGH)
    back = back.reshape(2, SIDE, 4, SIDE).transpose(2, 1, 0, 3).reshape(4 * SIDE, 2 * SIDE)
    g = lax.dot_general(back, fwd, (((1,), (1,)), ((), ())), precision=HIGH).reshape(4, SIDE, 2, SIDE)
    gr, gi = g[:, :, 0], g[:, :, 1]
    qr, qi = tr * gr + ti * gi, tr * gi - ti * gr
    grads = [
        jnp.sum(pr * qi - pi * qr, axis=0),
        -jnp.sum(pr * qr + pi * qi, axis=0),
    ]

    d_col = sum(jnp.sum(g_ * (w[2:, 1:-1] - w[:-2, 1:-1])) for g_, w in zip(grads, wins))
    d_row = sum(jnp.sum(g_ * (w[1:-1, 2:] - w[1:-1, :-2])) for g_, w in zip(grads, wins))
    locus = (jnp.stack([d_col, d_row]) * (0.5 / SIDE))[None, None]

    terms = jnp.stack([qr, qi], axis=1).reshape(NA, SIDE, SIDE)
    piece = exchange(terms, ANGLE).sum(0).reshape(64, 8, 128)
    piece = exchange(piece, SLAB).sum(0)
    probe_grad = lax.all_gather(piece, ANGLE, axis=0, tiled=False).reshape(4, 2, 4, SIDE)

    pad = DET - SIDE
    placed = jnp.concatenate(
        [
            lax.dynamic_slice(jnp.pad(g_, pad), (pad - col, pad - row), (DET, DET))
            for g_ in grads
        ],
        axis=1,
    )
    placed = placed.reshape(NUB, NY, QC, LANES).transpose(1, 0, 2, 3).reshape(DET, LANES)
    part = exchange(to_tiles(placed).reshape(NY, 50, 8, 128), "y").sum(0)
    quarter = from_tiles(sum_over_z(part)).reshape(NUB, QC, LANES)
    sent = quarter[0][None]
    for d in range(1, NUB):
        sent = jnp.where((ids == d)[:, None, None], quarter[d][None], sent)
    blocks = exchange(sent, ("y", "x", "core")).reshape(512, LANES)
    vol = lax.dot_general(
        kern.astype(jnp.float32), blocks, (((0,), (0,)), ((), ())), precision=HIGH
    )
    vol_grad = vol.reshape(128, 2, DET).transpose(1, 0, 2).reshape(2, 8, 16, DET)
    return vol_grad, probe_grad, resid[None, None], locus


def solution(mesh):
    mesh = Mesh(mesh.devices.reshape(NY, NZ, NX, NC), ("y", "z", "x", "core"))
    in_specs = (
        P(None, SLAB, ANGLE, None),
        P(),
        P(),
        P(),
        P(ANGLE, SLAB, None),
        P(ANGLE, SLAB, None, None),
    )
    out_specs = (
        P(None, SLAB, ANGLE, None),
        P(None, None, SLAB, None),
        P(ANGLE, SLAB, None, None),
        P(ANGLE, SLAB, None),
    )
    return jax.shard_map(local, mesh=mesh, in_specs=in_specs, out_specs=out_specs, check_vma=False)
```

```python
import numpy as np

import jax
import jax.numpy as jnp
from jax import lax
from jax.experimental import pallas as pl
from jax.experimental.pallas import tpu as pltpu
from jax.sharding import Mesh
from jax.sharding import PartitionSpec as P

NY, NZ, NX, NC = 4, 16, 4, 2
NA = NX * NC
NUB, UB, SIDE, DET = 5, 64, 256, 320
QC = UB // NY
LANES = 2 * DET
SLAB = ("y", "z")
ANGLE = ("x", "core")
HIGH = lax.Precision.HIGH


def dft_tables():
    k = np.arange(SIDE)
    ph = (k[:, None] * k[None, :] % SIDE) * (2.0 * np.pi / SIDE)
    c, s = np.cos(ph) / np.sqrt(SIDE), np.sin(ph) / np.sqrt(SIDE)
    both = np.stack([c, s, -s])
    hi = both.astype(jnp.bfloat16)
    lo = (both - hi.astype(np.float64)).astype(jnp.bfloat16)
    return np.concatenate([hi, lo])


def split(v):
    hi = v.astype(jnp.bfloat16)
    return hi, (v - hi.astype(jnp.float32)).astype(jnp.bfloat16)


def dot(a, b):
    return jnp.dot(a, b, preferred_element_type=jnp.float32)


def times(v, hi, lo):
    vh, vl = split(v)
    return dot(vh, hi) + dot(vl, hi) + dot(vh, lo)


def of(hi, lo, v):
    vh, vl = split(v)
    return dot(hi, vh) + dot(hi, vl) + dot(lo, vh)


def spot_kernel(core_ref, tr_ref, ti_ref, probe_ref, power_ref, tab_ref, resid_ref, keep_ref, send_ref, grads_ref, far_ref, big_ref):
    for k in range(2):
        for t in range(2):
            for i in range(2):
                for j in range(2):
                    of_s = 0 if i == j else (1 if (i > j) == (t == 0) else 2)
                    big_ref[2 * t + k, i * SIDE : (i + 1) * SIDE, j * SIDE : (j + 1) * SIDE] = tab_ref[3 * k + of_s]
    fwd, bwd = (big_ref[0], big_ref[1]), (big_ref[2], big_ref[3])
    first = core_ref[0] == 0
    resid_ref[...] = -power_ref[...]
    for m in range(4):
        tr, ti = tr_ref[...], ti_ref[...]
        pr, pi = (probe_ref[2 * m + k].astype(jnp.float32) for k in range(2))
        mid = times(jnp.concatenate([pr * tr - pi * ti, pr * ti + pi * tr], axis=1), *fwd)
        far = of(*bwd, jnp.concatenate([mid[:, :SIDE], mid[:, SIDE:]], axis=0))
        far_ref[m] = far
        resid_ref[...] += far[:SIDE] * far[:SIDE] + far[SIDE:] * far[SIDE:]
    grads_ref[...] = jnp.zeros_like(grads_ref)
    for m in range(4):
        tr, ti = tr_ref[...], ti_ref[...]
        pr, pi = (probe_ref[2 * m + k].astype(jnp.float32) for k in range(2))
        twice, far = 2.0 * resid_ref[...], far_ref[m]
        back = of(*fwd, jnp.concatenate([far[:SIDE] * twice, far[SIDE:] * twice], axis=0))
        g = times(jnp.concatenate([back[:SIDE], back[SIDE:]], axis=1), *bwd)
        gr, gi = g[:, :SIDE], g[:, SIDE:]
        qr, qi = tr * gr + ti * gi, tr * gi - ti * gr
        keep_ref[m] = jnp.where(first, qr, qi)
        send_ref[m] = jnp.where(first, qi, qr)
        grads_ref[0] += pr * qi - pi * qr
        grads_ref[1] -= pr * qr + pi * qi


def spot(core, tr, ti, probe, power, tab):
    f32 = jnp.float32
    plane = jax.ShapeDtypeStruct((SIDE, SIDE), f32)
    half = jax.ShapeDtypeStruct((4, SIDE, SIDE), f32)
    vmem = pl.BlockSpec(memory_space=pltpu.VMEM)
    return pl.pallas_call(
        spot_kernel,
        out_shape=(plane, half, half, jax.ShapeDtypeStruct((2, SIDE, SIDE), f32)),
        in_specs=[pl.BlockSpec(memory_space=pltpu.SMEM)] + [vmem] * 5,
        out_specs=(vmem,) * 4,
        scratch_shapes=[
            pltpu.VMEM((4, 2 * SIDE, SIDE), f32),
            pltpu.VMEM((4, 2 * SIDE, 2 * SIDE), jnp.bfloat16),
        ],
        name="spot",
    )(core, tr, ti, probe, power, tab)


def exchange(x, axes):
    return lax.all_to_all(x, axes, split_axis=0, concat_axis=0, tiled=True)


def to_tiles(q):
    n = q.shape[0] // 8
    return q.reshape(n, 8, 5, 128).transpose(0, 2, 1, 3).reshape(n * 5, 8, 128)


def from_tiles(t):
    n = t.shape[0] // 5
    return t.reshape(n, 5, 8, 128).transpose(0, 2, 1, 3).reshape(n * 8, LANES)


def sum_over_z(tiles):
    padded = jnp.pad(tiles, ((0, 14), (0, 0), (0, 0))).reshape(NZ, 4, 8, 128)
    return exchange(padded, "z").sum(0)


def shift(x, axis, size, by):
    return lax.ppermute(x, axis, [(i, (i + by) % size) for i in range(size)])


def step(volume, matrices, tile_ids, modes, corners, power):
    y, z = lax.axis_index("y"), lax.axis_index("z")
    angle = lax.axis_index(ANGLE)
    tile = volume.reshape(2, 128, DET).transpose(1, 0, 2).reshape(128, LANES)
    kern = matrices.reshape(NA, NY, QC, 128).transpose(1, 0, 2, 3).reshape(512, 128)
    ids = lax.dynamic_index_in_dim(tile_ids, angle, 0, keepdims=False)
    ids = lax.dynamic_index_in_dim(ids.reshape(NY, NZ, NA), z, 1, keepdims=False).reshape(32)

    rays = jnp.dot(kern, tile, preferred_element_type=jnp.float32).reshape(32, QC, LANES)
    items = exchange(rays, ("y", "x", "core"))
    quarter = jnp.stack(
        [jnp.sum(jnp.where((ids == d)[:, None, None], items, 0.0), axis=0) for d in range(NUB)]
    )
    mine = sum_over_z(to_tiles(quarter.reshape(NUB * QC, LANES)))
    copies = jnp.broadcast_to(mine[None], (NZ, 4, 8, 128))
    summed = exchange(copies, "z").reshape(64, 8, 128)[:50]
    every = lax.all_gather(summed, "y", axis=0, tiled=False)
    det = from_tiles(every.reshape(200, 8, 128))
    det = det.reshape(NY, NUB, QC, LANES).transpose(1, 0, 2, 3).reshape(DET, LANES)

    col, row = corners[0, 0, 0], corners[0, 0, 1]
    wins = [lax.dynamic_slice(det, (col - 1, k * DET + row - 1), (SIDE + 2, SIDE + 2)) for k in range(2)]
    p0, p1 = wins[0][1:-1, 1:-1], wins[1][1:-1, 1:-1]
    absorb = jnp.exp(-p1)
    tr, ti = absorb * jnp.cos(p0), absorb * jnp.sin(p0)
    core = lax.axis_index("core")
    resid, keep, send, grads = spot(
        core.reshape(1), tr, ti, modes.reshape(8, SIDE, SIDE), power[0, 0], jnp.asarray(dft_tables())
    )

    d_col = sum(jnp.sum(g_ * (w[2:, 1:-1] - w[:-2, 1:-1])) for g_, w in zip((grads[0], grads[1]), wins))
    d_row = sum(jnp.sum(g_ * (w[1:-1, 2:] - w[1:-1, :-2])) for g_, w in zip((grads[0], grads[1]), wins))
    locus = (jnp.stack([d_col, d_row]) * (0.5 / SIDE))[None, None]

    planes = keep + shift(send, "core", NC, 1)
    planes = exchange(planes, "x")
    piece = planes.sum(0).reshape(64, 8, 128)
    piece = exchange(piece, SLAB)
    piece = piece.sum(0)
    probe_grad = lax.all_gather(piece, ANGLE, axis=0, tiled=False).reshape(4, 2, 4, SIDE)

    pad = DET - SIDE
    placed = jnp.concatenate(
        [
            lax.dynamic_slice(jnp.pad(g_, pad), (pad - col, pad - row), (DET, DET))
            for g_ in (grads[0], grads[1])
        ],
        axis=1,
    )
    placed = placed.reshape(NUB, NY, QC, LANES).transpose(1, 0, 2, 3).reshape(DET, LANES)
    placed = to_tiles(placed).reshape(NY, 50, 8, 128)
    part = lax.dynamic_index_in_dim(placed, y, 0, keepdims=False)
    for k in (2, 1, 3):
        part += shift(lax.dynamic_index_in_dim(placed, (y + k) % NY, 0, keepdims=False), "y", NY, k)
    mine = sum_over_z(part)
    quarter = lax.all_gather(mine, "z", axis=0, tiled=True)
    quarter = from_tiles(quarter[:50]).reshape(NUB, QC, LANES)
    sent = quarter[0][None]
    for d in range(1, NUB):
        sent = jnp.where((ids == d)[:, None, None], quarter[d][None], sent)
    blocks = exchange(sent, ("y", "x", "core")).reshape(512, LANES)
    vol = lax.dot_general(
        kern.astype(jnp.float32), blocks, (((0,), (0,)), ((), ())), precision=HIGH
    )
    vol_grad = vol.reshape(128, 2, DET).transpose(1, 0, 2).reshape(2, 8, 16, DET)
    return vol_grad, probe_grad, resid[None, None], locus


def solution(mesh):
    mesh = Mesh(mesh.devices.reshape(NY, NZ, NX, NC), ("y", "z", "x", "core"))
    in_specs = (
        P(None, SLAB, ANGLE, None),
        P(),
        P(),
        P(),
        P(ANGLE, SLAB, None),
        P(ANGLE, SLAB, None, None),
    )
    out_specs = (
        P(None, SLAB, ANGLE, None),
        P(None, None, SLAB, None),
        P(ANGLE, SLAB, None, None),
        P(ANGLE, SLAB, None),
    )
    return jax.shard_map(step, mesh=mesh, in_specs=in_specs, out_specs=out_specs, check_vma=False)
```

```python
import numpy as np

import jax
import jax.numpy as jnp
from jax import lax
from jax.experimental import pallas as pl
from jax.experimental.pallas import tpu as pltpu
from jax.sharding import Mesh
from jax.sharding import PartitionSpec as P

NY, NZ, NX, NC = 4, 16, 4, 2
NA = NX * NC
NUB, UB, SIDE, DET = 5, 64, 256, 320
QC = UB // NY
LANES = 2 * DET
LIMIT = 16 << 20
SLAB = ("y", "z")
ANGLE = ("x", "core")
HIGH = lax.Precision.HIGH


def dft_tables():
    k = np.arange(SIDE)
    ph = (k[:, None] * k[None, :] % SIDE) * (2.0 * np.pi / SIDE)
    c, s = np.cos(ph) / np.sqrt(SIDE), np.sin(ph) / np.sqrt(SIDE)
    both = np.stack([c, s, -s])
    hi = both.astype(jnp.bfloat16)
    lo = (both - hi.astype(np.float64)).astype(jnp.bfloat16)
    return np.concatenate([hi, lo])


def split(v):
    hi = v.astype(jnp.bfloat16)
    return hi, (v - hi.astype(jnp.float32)).astype(jnp.bfloat16)


def dot(a, b):
    return jnp.dot(a, b, preferred_element_type=jnp.float32)


def times(v, hi, lo):
    vh, vl = split(v)
    return dot(vh, hi) + dot(vl, hi) + dot(vh, lo)


def of(hi, lo, v):
    vh, vl = split(v)
    return dot(hi, vh) + dot(hi, vl) + dot(lo, vh)


def spot_kernel(where_ref, tr_ref, ti_ref, probe_ref, power_ref, tab_ref, resid_ref, keep_ref, send_ref, grads_ref, placed_ref, far_ref, big_ref, det_ref):
    for k in range(2):
        for t in range(2):
            for i in range(2):
                for j in range(2):
                    of_s = 0 if i == j else (1 if (i > j) == (t == 0) else 2)
                    big_ref[2 * t + k, i * SIDE : (i + 1) * SIDE, j * SIDE : (j + 1) * SIDE] = tab_ref[3 * k + of_s]
    fwd, bwd = (big_ref[0], big_ref[1]), (big_ref[2], big_ref[3])
    first = where_ref[0] == 0
    resid_ref[...] = -power_ref[...]
    for m in range(4):
        tr, ti = tr_ref[...], ti_ref[...]
        pr, pi = (probe_ref[2 * m + k].astype(jnp.float32) for k in range(2))
        mid = times(jnp.concatenate([pr * tr - pi * ti, pr * ti + pi * tr], axis=1), *fwd)
        far = of(*bwd, jnp.concatenate([mid[:, :SIDE], mid[:, SIDE:]], axis=0))
        far_ref[m] = far
        resid_ref[...] += far[:SIDE] * far[:SIDE] + far[SIDE:] * far[SIDE:]
    grads_ref[...] = jnp.zeros_like(grads_ref)
    for m in range(4):
        tr, ti = tr_ref[...], ti_ref[...]
        pr, pi = (probe_ref[2 * m + k].astype(jnp.float32) for k in range(2))
        twice, far = 2.0 * resid_ref[...], far_ref[m]
        back = of(*fwd, jnp.concatenate([far[:SIDE] * twice, far[SIDE:] * twice], axis=0))
        g = times(jnp.concatenate([back[:SIDE], back[SIDE:]], axis=1), *bwd)
        gr, gi = g[:, :SIDE], g[:, SIDE:]
        qr, qi = tr * gr + ti * gi, tr * gi - ti * gr
        keep_ref[m] = jnp.where(first, qr, qi)
        send_ref[m] = jnp.where(first, qi, qr)
        grads_ref[0] += pr * qi - pi * qr
        grads_ref[1] -= pr * qr + pi * qi
    col, row = where_ref[1], where_ref[2]
    blank = jnp.zeros((SIDE, 128), jnp.float32)
    g0 = pltpu.roll(jnp.concatenate([grads_ref[0], blank], axis=1), row, 1)
    g1 = pltpu.roll(jnp.concatenate([grads_ref[1], blank], axis=1), row + 64, 1)
    det_ref[...] = jnp.zeros_like(det_ref)
    wide = jnp.concatenate([g0[:, :256], g0[:, 256:] + g1[:, :128], g1[:, 128:]], axis=1)
    wide = jnp.concatenate([wide, jnp.zeros((8, LANES), jnp.float32)], axis=0)
    start = pl.multiple_of((col >> 3) << 3, 8)
    det_ref[pl.ds(start, SIDE + 8), :] = pltpu.roll(wide, col & 7, 0)
    for y in range(NY):
        for g in range(10):
            at = (g // 2) * UB + y * QC + (g % 2) * 8
            for t in range(5):
                placed_ref[y, g * 5 + t] = det_ref[at : at + 8, t * 128 : (t + 1) * 128]


def spot(where, tr, ti, probe, power, tab):
    f32 = jnp.float32
    plane = jax.ShapeDtypeStruct((SIDE, SIDE), f32)
    half = jax.ShapeDtypeStruct((4, SIDE, SIDE), f32)
    vmem = pl.BlockSpec(memory_space=pltpu.VMEM)
    return pl.pallas_call(
        spot_kernel,
        out_shape=(
            plane,
            half,
            half,
            jax.ShapeDtypeStruct((2, SIDE, SIDE), f32),
            jax.ShapeDtypeStruct((NY, 50, 8, 128), f32),
        ),
        in_specs=[pl.BlockSpec(memory_space=pltpu.SMEM)] + [vmem] * 5,
        out_specs=(vmem,) * 5,
        scratch_shapes=[
            pltpu.VMEM((4, 2 * SIDE, SIDE), f32),
            pltpu.VMEM((4, 2 * SIDE, 2 * SIDE), jnp.bfloat16),
            pltpu.VMEM((DET, LANES), f32),
        ],
        compiler_params=pltpu.CompilerParams(vmem_limit_bytes=LIMIT),
        name="spot",
    )(where, tr, ti, probe, power, tab)


def exchange(x, axes):
    return lax.all_to_all(x, axes, split_axis=0, concat_axis=0, tiled=True)


def to_tiles(q):
    n = q.shape[0] // 8
    return q.reshape(n, 8, 5, 128).transpose(0, 2, 1, 3).reshape(n * 5, 8, 128)


def from_tiles(t):
    n = t.shape[0] // 5
    return t.reshape(n, 5, 8, 128).transpose(0, 2, 1, 3).reshape(n * 8, LANES)


def chunks_of_z(tiles):
    return jnp.pad(tiles, ((0, 14), (0, 0), (0, 0))).reshape(NZ, 4, 8, 128)


def pick(x, i, n):
    return lax.dynamic_index_in_dim(x, i % n, 0, keepdims=False)


def shift(x, axis, size, by):
    return lax.ppermute(x, axis, [(i, (i + by) % size) for i in range(size)])


def step(volume, matrices, tile_ids, modes, corners, power):
    y, z = lax.axis_index("y"), lax.axis_index("z")
    angle = lax.axis_index(ANGLE)
    tile = volume.reshape(2, 128, DET).transpose(1, 0, 2).reshape(128, LANES)
    kern = matrices.reshape(NA, NY, QC, 128).transpose(1, 0, 2, 3).reshape(512, 128)
    ids = lax.dynamic_index_in_dim(tile_ids, angle, 0, keepdims=False)
    ids = lax.dynamic_index_in_dim(ids.reshape(NY, NZ, NA), z, 1, keepdims=False).reshape(32)

    rays = jnp.dot(kern, tile, preferred_element_type=jnp.float32).reshape(32, QC, LANES)
    items = exchange(rays, ("y", "x", "core"))
    quarter = jnp.stack(
        [jnp.sum(jnp.where((ids == d)[:, None, None], items, 0.0), axis=0) for d in range(NUB)]
    )
    mine = exchange(chunks_of_z(to_tiles(quarter.reshape(NUB * QC, LANES))), "z").sum(0)
    copies = jnp.broadcast_to(mine[None], (NZ, 4, 8, 128))
    summed = exchange(copies, "z").reshape(64, 8, 128)[:50]
    every = lax.all_gather(summed, "y", axis=0, tiled=False)
    det = from_tiles(every.reshape(200, 8, 128))
    det = det.reshape(NY, NUB, QC, LANES).transpose(1, 0, 2, 3).reshape(DET, LANES)

    col, row = corners[0, 0, 0], corners[0, 0, 1]
    wins = [lax.dynamic_slice(det, (col - 1, k * DET + row - 1), (SIDE + 2, SIDE + 2)) for k in range(2)]
    p0, p1 = wins[0][1:-1, 1:-1], wins[1][1:-1, 1:-1]
    absorb = jnp.exp(-p1)
    tr, ti = absorb * jnp.cos(p0), absorb * jnp.sin(p0)
    core = lax.axis_index("core")
    resid, keep, send, grads, placed = spot(
        jnp.stack([core, col, row]), tr, ti, modes.reshape(8, SIDE, SIDE), power[0, 0], jnp.asarray(dft_tables())
    )

    d_col = sum(jnp.sum(g_ * (w[2:, 1:-1] - w[:-2, 1:-1])) for g_, w in zip((grads[0], grads[1]), wins))
    d_row = sum(jnp.sum(g_ * (w[1:-1, 2:] - w[1:-1, :-2])) for g_, w in zip((grads[0], grads[1]), wins))
    locus = (jnp.stack([d_col, d_row]) * (0.5 / SIDE))[None, None]

    other = shift(send, "core", NC, 1)
    planes = keep + other
    got = [shift(pick(planes, lax.axis_index("x") + k, NX), "x", NX, k) for k in (2, 1, 3)]
    rows = (pick(planes, lax.axis_index("x"), NX) + got[0] + got[1] + got[2]).reshape(NY, 64, SIDE)
    got = [shift(pick(rows, y + k, NY), "y", NY, k) for k in (2, 1, 3)]
    rows = (pick(rows, y, NY) + got[0] + got[1] + got[2]).reshape(NZ, 1, 8, 128)

    part = exchange(placed, "y")
    part = part.sum(0)
    part = exchange(chunks_of_z(part), "z")
    mine = part.sum(0)
    got = exchange(jnp.concatenate([jnp.broadcast_to(mine[None], (NZ, 4, 8, 128)), rows], axis=1), "z")
    piece = got[:, 4].sum(0)
    quarter = got[:, :4].reshape(64, 8, 128)[:50].reshape(NUB, 10, 8, 128)
    sent = quarter[0][None]
    for d in range(1, NUB):
        sent = jnp.where((ids == d)[:, None, None, None], quarter[d][None], sent)
    sent = jnp.concatenate([sent, jnp.broadcast_to(piece[None, None], (32, 1, 8, 128))], axis=1)
    got = exchange(sent, ("y", "x", "core"))
    probe_grad = lax.dynamic_slice_in_dim(got[:, 10], y * NA, NA, 0).reshape(4, 2, 4, SIDE)
    blocks = from_tiles(got[:, :10].reshape(320, 8, 128))
    vol = lax.dot_general(
        kern.astype(jnp.float32), blocks, (((0,), (0,)), ((), ())), precision=HIGH
    )
    vol_grad = vol.reshape(128, 2, DET).transpose(1, 0, 2).reshape(2, 8, 16, DET)
    return vol_grad, probe_grad, resid[None, None], locus


def solution(mesh):
    mesh = Mesh(mesh.devices.reshape(NY, NZ, NX, NC), ("y", "z", "x", "core"))
    in_specs = (
        P(None, SLAB, ANGLE, None),
        P(),
        P(),
        P(),
        P(ANGLE, SLAB, None),
        P(ANGLE, SLAB, None, None),
    )
    out_specs = (
        P(None, SLAB, ANGLE, None),
        P(None, None, SLAB, None),
        P(ANGLE, SLAB, None, None),
        P(ANGLE, SLAB, None),
    )
    return jax.shard_map(step, mesh=mesh, in_specs=in_specs, out_specs=out_specs, check_vma=False)
```

```python
import numpy as np

import jax
import jax.numpy as jnp
from jax import lax
from jax.experimental import pallas as pl
from jax.experimental.pallas import tpu as pltpu
from jax.sharding import Mesh
from jax.sharding import PartitionSpec as P

NY, NZ, NX, NC = 4, 16, 4, 2
NA = NX * NC
NUB, UB, SIDE, DET = 5, 64, 256, 320
QC = UB // NY
LANES = 2 * DET
LIMIT = 16 << 20
SLAB = ("y", "z")
ANGLE = ("x", "core")


def dft_tables():
    k = np.arange(SIDE)
    ph = (k[:, None] * k[None, :] % SIDE) * (2.0 * np.pi / SIDE)
    c, s = np.cos(ph) / np.sqrt(SIDE), np.sin(ph) / np.sqrt(SIDE)
    both = np.stack([c, s, -s])
    hi = both.astype(jnp.bfloat16)
    lo = (both - hi.astype(np.float64)).astype(jnp.bfloat16)
    return np.concatenate([hi, lo])


def split(v):
    hi = v.astype(jnp.bfloat16)
    return hi, (v - hi.astype(jnp.float32)).astype(jnp.bfloat16)


def dot(a, b):
    return jnp.dot(a, b, preferred_element_type=jnp.float32)


def times(v, hi, lo):
    vh, vl = split(v)
    return dot(vh, hi) + dot(vl, hi) + dot(vh, lo)


def of(hi, lo, v):
    vh, vl = split(v)
    return dot(hi, vh) + dot(hi, vl) + dot(lo, vh)


def spot_kernel(where_ref, tr_ref, ti_ref, probe_ref, power_ref, tab_ref, resid_ref, keep_ref, send_ref, grads_ref, placed_ref, far_ref, big_ref, det_ref):
    for k in range(2):
        for t in range(2):
            for i in range(2):
                for j in range(2):
                    of_s = 0 if i == j else (1 if (i > j) == (t == 0) else 2)
                    big_ref[2 * t + k, i * SIDE : (i + 1) * SIDE, j * SIDE : (j + 1) * SIDE] = tab_ref[3 * k + of_s]
    fwd, bwd = (big_ref[0], big_ref[1]), (big_ref[2], big_ref[3])
    first = where_ref[0] == 0
    resid_ref[...] = -power_ref[...]
    for m in range(4):
        tr, ti = tr_ref[...], ti_ref[...]
        pr, pi = (probe_ref[2 * m + k].astype(jnp.float32) for k in range(2))
        mid = times(jnp.concatenate([pr * tr - pi * ti, pr * ti + pi * tr], axis=1), *fwd)
        far = of(*bwd, jnp.concatenate([mid[:, :SIDE], mid[:, SIDE:]], axis=0))
        far_ref[m] = far
        resid_ref[...] += far[:SIDE] * far[:SIDE] + far[SIDE:] * far[SIDE:]
    grads_ref[...] = jnp.zeros_like(grads_ref)
    for m in range(4):
        tr, ti = tr_ref[...], ti_ref[...]
        pr, pi = (probe_ref[2 * m + k].astype(jnp.float32) for k in range(2))
        twice, far = 2.0 * resid_ref[...], far_ref[m]
        back = of(*fwd, jnp.concatenate([far[:SIDE] * twice, far[SIDE:] * twice], axis=0))
        g = times(jnp.concatenate([back[:SIDE], back[SIDE:]], axis=1), *bwd)
        gr, gi = g[:, :SIDE], g[:, SIDE:]
        qr, qi = tr * gr + ti * gi, tr * gi - ti * gr
        keep_ref[m] = jnp.where(first, qr, qi)
        send_ref[m] = jnp.where(first, qi, qr)
        grads_ref[0] += pr * qi - pi * qr
        grads_ref[1] -= pr * qr + pi * qi
    col, row = where_ref[1], where_ref[2]
    blank = jnp.zeros((SIDE, 128), jnp.float32)
    g0 = pltpu.roll(jnp.concatenate([grads_ref[0], blank], axis=1), row, 1)
    g1 = pltpu.roll(jnp.concatenate([grads_ref[1], blank], axis=1), row + 64, 1)
    det_ref[...] = jnp.zeros_like(det_ref)
    wide = jnp.concatenate([g0[:, :256], g0[:, 256:] + g1[:, :128], g1[:, 128:]], axis=1)
    wide = jnp.concatenate([wide, jnp.zeros((8, LANES), jnp.float32)], axis=0)
    start = pl.multiple_of((col >> 3) << 3, 8)
    det_ref[pl.ds(start, SIDE + 8), :] = pltpu.roll(wide, col & 7, 0)
    for y in range(NY):
        for g in range(10):
            at = (g // 2) * UB + y * QC + (g % 2) * 8
            for t in range(5):
                placed_ref[y, g * 5 + t] = det_ref[at : at + 8, t * 128 : (t + 1) * 128]


def spot(where, tr, ti, probe, power, tab):
    f32 = jnp.float32
    plane = jax.ShapeDtypeStruct((SIDE, SIDE), f32)
    half = jax.ShapeDtypeStruct((4, SIDE, SIDE), f32)
    vmem = pl.BlockSpec(memory_space=pltpu.VMEM)
    return pl.pallas_call(
        spot_kernel,
        out_shape=(
            plane,
            half,
            half,
            jax.ShapeDtypeStruct((2, SIDE, SIDE), f32),
            jax.ShapeDtypeStruct((NY, 50, 8, 128), f32),
        ),
        in_specs=[pl.BlockSpec(memory_space=pltpu.SMEM)] + [vmem] * 5,
        out_specs=(vmem,) * 5,
        scratch_shapes=[
            pltpu.VMEM((4, 2 * SIDE, SIDE), f32),
            pltpu.VMEM((4, 2 * SIDE, 2 * SIDE), jnp.bfloat16),
            pltpu.VMEM((DET, LANES), f32),
        ],
        compiler_params=pltpu.CompilerParams(vmem_limit_bytes=LIMIT),
        name="spot",
    )(where, tr, ti, probe, power, tab)


def rays_kernel(vol_ref, mat_ref, out_ref, tile_ref):
    tile_ref[:, :DET] = vol_ref[0].astype(jnp.float32)
    tile_ref[:, DET:] = vol_ref[1].astype(jnp.float32)
    tile = tile_ref[...].astype(jnp.bfloat16)
    for a in range(NA):
        sums = dot(mat_ref[a], tile)
        for y in range(NY):
            out_ref[y * NA + a] = sums[y * QC : (y + 1) * QC]


def rays_of(volume, matrices):
    vmem = pl.BlockSpec(memory_space=pltpu.VMEM)
    return pl.pallas_call(
        rays_kernel,
        out_shape=jax.ShapeDtypeStruct((32, QC, LANES), jnp.float32),
        in_specs=[vmem] * 2,
        out_specs=vmem,
        scratch_shapes=[pltpu.VMEM((128, LANES), jnp.float32)],
        compiler_params=pltpu.CompilerParams(vmem_limit_bytes=LIMIT),
        name="rays",
    )(volume, matrices)


def volume_kernel(y_ref, got_ref, mat_ref, vol_ref, probe_ref, hi_ref, lo_ref):
    for a in range(NA):
        for y in range(NY):
            at = a * UB + y * QC
            for t in range(5):
                v = jnp.concatenate([got_ref[y * NA + a, t], got_ref[y * NA + a, 5 + t]], axis=0)
                hi, lo = split(v)
                hi_ref[at : at + QC, t * 128 : (t + 1) * 128] = hi
                lo_ref[at : at + QC, t * 128 : (t + 1) * 128] = lo
    back = lambda ref: lax.dot_general(
        mat_ref[...], ref[...], (((0,), (0,)), ((), ())), preferred_element_type=jnp.float32
    )
    grad = back(hi_ref) + back(lo_ref)
    vol_ref[0] = grad[:, :DET]
    vol_ref[1] = pltpu.roll(grad, DET, 1)[:, :DET]
    for a in range(NA):
        piece = got_ref[y_ref[0] * NA + a, 10]
        for r in range(4):
            for k in range(2):
                probe_ref[a, r : r + 1, k * 128 : (k + 1) * 128] = piece[2 * r + k : 2 * r + k + 1]


def volume_of(y, got, matrices):
    vmem = pl.BlockSpec(memory_space=pltpu.VMEM)
    return pl.pallas_call(
        volume_kernel,
        out_shape=(
            jax.ShapeDtypeStruct((2, 128, DET), jnp.float32),
            jax.ShapeDtypeStruct((NA, 4, SIDE), jnp.float32),
        ),
        in_specs=[pl.BlockSpec(memory_space=pltpu.SMEM)] + [vmem] * 2,
        out_specs=(vmem,) * 2,
        scratch_shapes=[pltpu.VMEM((512, LANES), jnp.bfloat16)] * 2,
        compiler_params=pltpu.CompilerParams(vmem_limit_bytes=LIMIT),
        name="volume",
    )(y, got, matrices)


def exchange(x, axes):
    return lax.all_to_all(x, axes, split_axis=0, concat_axis=0, tiled=True)


def to_tiles(q):
    n = q.shape[0] // 8
    return q.reshape(n, 8, 5, 128).transpose(0, 2, 1, 3).reshape(n * 5, 8, 128)


def from_tiles(t):
    n = t.shape[0] // 5
    return t.reshape(n, 5, 8, 128).transpose(0, 2, 1, 3).reshape(n * 8, LANES)


def chunks_of_z(tiles):
    return tiles.reshape(NZ, 25, 1, 128)


def pick(x, i, n):
    return lax.dynamic_index_in_dim(x, i % n, 0, keepdims=False)


def shift(x, axis, size, by):
    return lax.ppermute(x, axis, [(i, (i + by) % size) for i in range(size)])


def step(volume, matrices, tile_ids, modes, corners, power):
    y, z = lax.axis_index("y"), lax.axis_index("z")
    angle = lax.axis_index(ANGLE)
    ids = lax.dynamic_index_in_dim(tile_ids, angle, 0, keepdims=False)
    ids = lax.dynamic_index_in_dim(ids.reshape(NY, NZ, NA), z, 1, keepdims=False).reshape(32)

    items = exchange(rays_of(volume.reshape(2, 128, DET), matrices), ("y", "x", "core"))
    quarter = jnp.stack(
        [jnp.sum(jnp.where((ids == d)[:, None, None], items, 0.0), axis=0) for d in range(NUB)]
    )
    mine = exchange(chunks_of_z(to_tiles(quarter.reshape(NUB * QC, LANES))), "z").sum(0)
    copies = jnp.broadcast_to(mine[None], (NZ, 25, 1, 128))
    summed = exchange(copies, "z").reshape(50, 8, 128)
    every = lax.all_gather(summed, "y", axis=0, tiled=False)
    det = from_tiles(every.reshape(200, 8, 128))
    det = det.reshape(NY, NUB, QC, LANES).transpose(1, 0, 2, 3).reshape(DET, LANES)

    col, row = corners[0, 0, 0], corners[0, 0, 1]
    wins = [lax.dynamic_slice(det, (col - 1, k * DET + row - 1), (SIDE + 2, SIDE + 2)) for k in range(2)]
    p0, p1 = wins[0][1:-1, 1:-1], wins[1][1:-1, 1:-1]
    absorb = jnp.exp(-p1)
    tr, ti = absorb * jnp.cos(p0), absorb * jnp.sin(p0)
    core = lax.axis_index("core")
    resid, keep, send, grads, placed = spot(
        jnp.stack([core, col, row]), tr, ti, modes.reshape(8, SIDE, SIDE), power[0, 0], jnp.asarray(dft_tables())
    )

    d_col = sum(jnp.sum(g_ * (w[2:, 1:-1] - w[:-2, 1:-1])) for g_, w in zip((grads[0], grads[1]), wins))
    d_row = sum(jnp.sum(g_ * (w[1:-1, 2:] - w[1:-1, :-2])) for g_, w in zip((grads[0], grads[1]), wins))
    locus = (jnp.stack([d_col, d_row]) * (0.5 / SIDE))[None, None]

    other = shift(send, "core", NC, 1)
    planes = keep + other
    got = [shift(pick(planes, lax.axis_index("x") + k, NX), "x", NX, k) for k in (2, 1, 3)]
    rows = (pick(planes, lax.axis_index("x"), NX) + got[0] + got[1] + got[2]).reshape(NY, 64, SIDE)
    got = [shift(pick(rows, y + k, NY), "y", NY, k) for k in (2, 1, 3)]
    rows = (pick(rows, y, NY) + got[0] + got[1] + got[2]).reshape(NZ, 8, 1, 128)

    part = exchange(placed, "y")
    part = part.sum(0)
    part = exchange(chunks_of_z(part), "z")
    mine = part.sum(0)
    got = exchange(jnp.concatenate([jnp.broadcast_to(mine[None], (NZ, 25, 1, 128)), rows], axis=1), "z")
    piece = got[:, 25:].sum(0).reshape(8, 128)
    quarter = got[:, :25].reshape(NUB, 10, 8, 128)
    sent = quarter[0][None]
    for d in range(1, NUB):
        sent = jnp.where((ids == d)[:, None, None, None], quarter[d][None], sent)
    sent = jnp.concatenate([sent, jnp.broadcast_to(piece[None, None], (32, 1, 8, 128))], axis=1)
    got = exchange(sent, ("y", "x", "core"))
    vol_grad, probe_grad = volume_of(y.reshape(1), got, matrices.reshape(512, 128))
    vol_grad = vol_grad.reshape(2, 8, 16, DET)
    probe_grad = probe_grad.reshape(4, 2, 4, SIDE)
    return vol_grad, probe_grad, resid[None, None], locus


def solution(mesh):
    mesh = Mesh(mesh.devices.reshape(NY, NZ, NX, NC), ("y", "z", "x", "core"))
    in_specs = (
        P(None, SLAB, ANGLE, None),
        P(),
        P(),
        P(),
        P(ANGLE, SLAB, None),
        P(ANGLE, SLAB, None, None),
    )
    out_specs = (
        P(None, SLAB, ANGLE, None),
        P(None, None, SLAB, None),
        P(ANGLE, SLAB, None, None),
        P(ANGLE, SLAB, None),
    )
    return jax.shard_map(step, mesh=mesh, in_specs=in_specs, out_specs=out_specs, check_vma=False)
```

```python
import numpy as np

import jax
import jax.numpy as jnp
from jax import lax
from jax.experimental import pallas as pl
from jax.experimental.pallas import tpu as pltpu
from jax.sharding import Mesh
from jax.sharding import PartitionSpec as P

NY, NZ, NX, NC = 4, 16, 4, 2
NA = NX * NC
NUB, UB, SIDE, DET = 5, 64, 256, 320
HALF = SIDE // 2
HIGHEST = lax.Precision.HIGHEST
QC = UB // NY
LANES = 2 * DET
LIMIT = 16 << 20
SLAB = ("y", "z")
ANGLE = ("x", "core")


def dft_tables():
    n, k = np.arange(HALF)[:, None], 2 * np.arange(HALF)[None, :]
    out = []
    for odd in range(2):
        ph = (n * (k + odd) % SIDE) * (2.0 * np.pi / SIDE)
        c, s = np.cos(ph) / np.sqrt(SIDE), np.sin(ph) / np.sqrt(SIDE)
        full = np.block([[c, -s], [s, c]])
        hi = full.astype(jnp.bfloat16)
        out += [hi, (full - hi.astype(np.float64)).astype(jnp.bfloat16)]
    return np.stack(out + [t.T for t in out])


def even_first():
    order = np.concatenate([np.arange(0, SIDE, 2), np.arange(1, SIDE, 2)])
    return np.eye(SIDE, dtype=np.float32)[order]


def split(v):
    hi = v.astype(jnp.bfloat16)
    return hi, (v - hi.astype(jnp.float32)).astype(jnp.bfloat16)


def dot(a, b):
    return jnp.dot(a, b, preferred_element_type=jnp.float32)


def times(v, hi, lo):
    vh, vl = split(v)
    return dot(vh, hi) + dot(vl, hi) + dot(vh, lo)


def of(hi, lo, v):
    vh, vl = split(v)
    return dot(hi, vh) + dot(hi, vl) + dot(lo, vh)


def lanes(*parts):
    return jnp.concatenate(parts, axis=1)


def rows(*parts):
    return jnp.concatenate(parts, axis=0)


def halves(v, axis):
    a, b = (v[:, :HALF], v[:, HALF:]) if axis else (v[:HALF], v[HALF:])
    return a + b, a - b


def spot_kernel(where_ref, tr_ref, ti_ref, probe_ref, power_ref, tab_ref, resid_ref, keep_ref, send_ref, grads_ref, placed_ref, far_ref, det_ref):
    even, odd, even_t, odd_t = ((tab_ref[2 * i], tab_ref[2 * i + 1]) for i in range(4))
    first = where_ref[0] == 0
    resid_ref[...] = -power_ref[...]
    for m in range(4):
        tr, ti = tr_ref[...], ti_ref[...]
        pr, pi = (probe_ref[2 * m + k].astype(jnp.float32) for k in range(2))
        sr, dr = halves(pr * tr - pi * ti, 1)
        si, di = halves(pr * ti + pi * tr, 1)
        me, mo = times(lanes(sr, si), *even), times(lanes(dr, di), *odd)
        sr, dr = halves(lanes(me[:, :HALF], mo[:, :HALF]), 0)
        si, di = halves(lanes(me[:, HALF:], mo[:, HALF:]), 0)
        fe, fo = of(*even_t, rows(sr, si)), of(*odd_t, rows(dr, di))
        far_ref[m, :SIDE] = fe
        far_ref[m, SIDE:] = fo
        resid_ref[...] += rows(fe[:HALF] * fe[:HALF] + fe[HALF:] * fe[HALF:], fo[:HALF] * fo[:HALF] + fo[HALF:] * fo[HALF:])
    grads_ref[...] = jnp.zeros_like(grads_ref)
    for m in range(4):
        tr, ti = tr_ref[...], ti_ref[...]
        pr, pi = (probe_ref[2 * m + k].astype(jnp.float32) for k in range(2))
        twice = 2.0 * resid_ref[...]
        te, to = twice[:HALF], twice[HALF:]
        be = of(*even, far_ref[m, :SIDE] * rows(te, te))
        bo = of(*odd, far_ref[m, SIDE:] * rows(to, to))
        top, bottom = be + bo, be - bo
        br, bi = rows(top[:HALF], bottom[:HALF]), rows(top[HALF:], bottom[HALF:])
        ge = times(lanes(br[:, :HALF], bi[:, :HALF]), *even_t)
        go = times(lanes(br[:, HALF:], bi[:, HALF:]), *odd_t)
        left, right = ge + go, ge - go
        gr, gi = lanes(left[:, :HALF], right[:, :HALF]), lanes(left[:, HALF:], right[:, HALF:])
        qr, qi = tr * gr + ti * gi, tr * gi - ti * gr
        keep_ref[m] = jnp.where(first, qr, qi)
        send_ref[m] = jnp.where(first, qi, qr)
        grads_ref[0] += pr * qi - pi * qr
        grads_ref[1] -= pr * qr + pi * qi
    col, row = where_ref[1], where_ref[2]
    blank = jnp.zeros((SIDE, 128), jnp.float32)
    g0 = pltpu.roll(jnp.concatenate([grads_ref[0], blank], axis=1), row, 1)
    g1 = pltpu.roll(jnp.concatenate([grads_ref[1], blank], axis=1), row + 64, 1)
    det_ref[...] = jnp.zeros_like(det_ref)
    wide = jnp.concatenate([g0[:, :256], g0[:, 256:] + g1[:, :128], g1[:, 128:]], axis=1)
    wide = jnp.concatenate([wide, jnp.zeros((8, LANES), jnp.float32)], axis=0)
    start = pl.multiple_of((col >> 3) << 3, 8)
    det_ref[pl.ds(start, SIDE + 8), :] = pltpu.roll(wide, col & 7, 0)
    for y in range(NY):
        for g in range(10):
            at = (g // 2) * UB + y * QC + (g % 2) * 8
            for t in range(5):
                placed_ref[y, g * 5 + t] = det_ref[at : at + 8, t * 128 : (t + 1) * 128]


def spot(where, tr, ti, probe, power, tab):
    f32 = jnp.float32
    plane = jax.ShapeDtypeStruct((SIDE, SIDE), f32)
    half = jax.ShapeDtypeStruct((4, SIDE, SIDE), f32)
    vmem = pl.BlockSpec(memory_space=pltpu.VMEM)
    return pl.pallas_call(
        spot_kernel,
        out_shape=(
            plane,
            half,
            half,
            jax.ShapeDtypeStruct((2, SIDE, SIDE), f32),
            jax.ShapeDtypeStruct((NY, 50, 8, 128), f32),
        ),
        in_specs=[pl.BlockSpec(memory_space=pltpu.SMEM)] + [vmem] * 5,
        out_specs=(vmem,) * 5,
        scratch_shapes=[
            pltpu.VMEM((4, 2 * SIDE, SIDE), f32),
            pltpu.VMEM((DET, LANES), f32),
        ],
        compiler_params=pltpu.CompilerParams(vmem_limit_bytes=LIMIT),
        name="spot",
    )(where, tr, ti, probe, power, tab)


def rays_kernel(vol_ref, mat_ref, out_ref, tile_ref):
    tile_ref[:, :DET] = vol_ref[0].astype(jnp.float32)
    tile_ref[:, DET:] = vol_ref[1].astype(jnp.float32)
    tile = tile_ref[...].astype(jnp.bfloat16)
    for a in range(NA):
        sums = dot(mat_ref[a], tile)
        for y in range(NY):
            out_ref[y * NA + a] = sums[y * QC : (y + 1) * QC]


def rays_of(volume, matrices):
    vmem = pl.BlockSpec(memory_space=pltpu.VMEM)
    return pl.pallas_call(
        rays_kernel,
        out_shape=jax.ShapeDtypeStruct((32, QC, LANES), jnp.float32),
        in_specs=[vmem] * 2,
        out_specs=vmem,
        scratch_shapes=[pltpu.VMEM((128, LANES), jnp.float32)],
        compiler_params=pltpu.CompilerParams(vmem_limit_bytes=LIMIT),
        name="rays",
    )(volume, matrices)


def volume_kernel(y_ref, got_ref, mat_ref, vol_ref, probe_ref, hi_ref, lo_ref):
    for a in range(NA):
        for y in range(NY):
            at = a * UB + y * QC
            for t in range(5):
                v = jnp.concatenate([got_ref[y * NA + a, t], got_ref[y * NA + a, 5 + t]], axis=0)
                hi, lo = split(v)
                hi_ref[at : at + QC, t * 128 : (t + 1) * 128] = hi
                lo_ref[at : at + QC, t * 128 : (t + 1) * 128] = lo
    back = lambda ref: lax.dot_general(
        mat_ref[...], ref[...], (((0,), (0,)), ((), ())), preferred_element_type=jnp.float32
    )
    grad = back(hi_ref) + back(lo_ref)
    vol_ref[0] = grad[:, :DET]
    vol_ref[1] = pltpu.roll(grad, DET, 1)[:, :DET]
    for a in range(NA):
        piece = got_ref[y_ref[0] * NA + a, 10]
        for r in range(4):
            for k in range(2):
                probe_ref[a, r : r + 1, k * 128 : (k + 1) * 128] = piece[2 * r + k : 2 * r + k + 1]


def volume_of(y, got, matrices):
    vmem = pl.BlockSpec(memory_space=pltpu.VMEM)
    return pl.pallas_call(
        volume_kernel,
        out_shape=(
            jax.ShapeDtypeStruct((2, 128, DET), jnp.float32),
            jax.ShapeDtypeStruct((NA, 4, SIDE), jnp.float32),
        ),
        in_specs=[pl.BlockSpec(memory_space=pltpu.SMEM)] + [vmem] * 2,
        out_specs=(vmem,) * 2,
        scratch_shapes=[pltpu.VMEM((512, LANES), jnp.bfloat16)] * 2,
        compiler_params=pltpu.CompilerParams(vmem_limit_bytes=LIMIT),
        name="volume",
    )(y, got, matrices)


def exchange(x, axes):
    return lax.all_to_all(x, axes, split_axis=0, concat_axis=0, tiled=True)


def to_tiles(q):
    n = q.shape[0] // 8
    return q.reshape(n, 8, 5, 128).transpose(0, 2, 1, 3).reshape(n * 5, 8, 128)


def from_tiles(t):
    n = t.shape[0] // 5
    return t.reshape(n, 5, 8, 128).transpose(0, 2, 1, 3).reshape(n * 8, LANES)


def chunks_of_z(tiles):
    return tiles.reshape(NZ, 25, 1, 128)


def pick(x, i, n):
    return lax.dynamic_index_in_dim(x, i % n, 0, keepdims=False)


def shift(x, axis, size, by):
    return lax.ppermute(x, axis, [(i, (i + by) % size) for i in range(size)])


def step(volume, matrices, tile_ids, modes, corners, power):
    y, z = lax.axis_index("y"), lax.axis_index("z")
    angle = lax.axis_index(ANGLE)
    ids = lax.dynamic_index_in_dim(tile_ids, angle, 0, keepdims=False)
    ids = lax.dynamic_index_in_dim(ids.reshape(NY, NZ, NA), z, 1, keepdims=False).reshape(32)

    items = exchange(rays_of(volume.reshape(2, 128, DET), matrices), ("y", "x", "core"))
    quarter = jnp.stack(
        [jnp.sum(jnp.where((ids == d)[:, None, None], items, 0.0), axis=0) for d in range(NUB)]
    )
    mine = exchange(chunks_of_z(to_tiles(quarter.reshape(NUB * QC, LANES))), "z").sum(0)
    copies = jnp.broadcast_to(mine[None], (NZ, 25, 1, 128))
    summed = exchange(copies, "z").reshape(50, 8, 128)
    every = lax.all_gather(summed, "y", axis=0, tiled=False)
    det = from_tiles(every.reshape(200, 8, 128))
    det = det.reshape(NY, NUB, QC, LANES).transpose(1, 0, 2, 3).reshape(DET, LANES)

    col, row = corners[0, 0, 0], corners[0, 0, 1]
    wins = [lax.dynamic_slice(det, (col - 1, k * DET + row - 1), (SIDE + 2, SIDE + 2)) for k in range(2)]
    p0, p1 = wins[0][1:-1, 1:-1], wins[1][1:-1, 1:-1]
    absorb = jnp.exp(-p1)
    tr, ti = absorb * jnp.cos(p0), absorb * jnp.sin(p0)
    core = lax.axis_index("core")
    order = jnp.asarray(even_first())
    turn = lambda p, v: jnp.dot(jnp.dot(p, v, precision=HIGHEST), p.T, precision=HIGHEST)
    resid, keep, send, grads, placed = spot(
        jnp.stack([core, col, row]), tr, ti, modes.reshape(8, SIDE, SIDE), turn(order, power[0, 0]), jnp.asarray(dft_tables())
    )
    resid = turn(order.T, resid)

    d_col = sum(jnp.sum(g_ * (w[2:, 1:-1] - w[:-2, 1:-1])) for g_, w in zip((grads[0], grads[1]), wins))
    d_row = sum(jnp.sum(g_ * (w[1:-1, 2:] - w[1:-1, :-2])) for g_, w in zip((grads[0], grads[1]), wins))
    locus = (jnp.stack([d_col, d_row]) * (0.5 / SIDE))[None, None]

    other = shift(send, "core", NC, 1)
    planes = keep + other
    got = [shift(pick(planes, lax.axis_index("x") + k, NX), "x", NX, k) for k in (2, 1, 3)]
    rows = (pick(planes, lax.axis_index("x"), NX) + got[0] + got[1] + got[2]).reshape(NY, 64, SIDE)
    got = [shift(pick(rows, y + k, NY), "y", NY, k) for k in (2, 1, 3)]
    rows = (pick(rows, y, NY) + got[0] + got[1] + got[2]).reshape(NZ, 8, 1, 128)

    part = exchange(placed, "y")
    part = part.sum(0)
    part = exchange(chunks_of_z(part), "z")
    mine = part.sum(0)
    got = exchange(jnp.concatenate([jnp.broadcast_to(mine[None], (NZ, 25, 1, 128)), rows], axis=1), "z")
    piece = got[:, 25:].sum(0).reshape(8, 128)
    quarter = got[:, :25].reshape(NUB, 10, 8, 128)
    sent = quarter[0][None]
    for d in range(1, NUB):
        sent = jnp.where((ids == d)[:, None, None, None], quarter[d][None], sent)
    sent = jnp.concatenate([sent, jnp.broadcast_to(piece[None, None], (32, 1, 8, 128))], axis=1)
    got = exchange(sent, ("y", "x", "core"))
    vol_grad, probe_grad = volume_of(y.reshape(1), got, matrices.reshape(512, 128))
    vol_grad = vol_grad.reshape(2, 8, 16, DET)
    probe_grad = probe_grad.reshape(4, 2, 4, SIDE)
    return vol_grad, probe_grad, resid[None, None], locus


def solution(mesh):
    mesh = Mesh(mesh.devices.reshape(NY, NZ, NX, NC), ("y", "z", "x", "core"))
    in_specs = (
        P(None, SLAB, ANGLE, None),
        P(),
        P(),
        P(),
        P(ANGLE, SLAB, None),
        P(ANGLE, SLAB, None, None),
    )
    out_specs = (
        P(None, SLAB, ANGLE, None),
        P(None, None, SLAB, None),
        P(ANGLE, SLAB, None, None),
        P(ANGLE, SLAB, None),
    )
    return jax.shard_map(step, mesh=mesh, in_specs=in_specs, out_specs=out_specs, check_vma=False)
```

```python
import numpy as np

import jax
import jax.numpy as jnp
from jax import lax
from jax.experimental import pallas as pl
from jax.experimental.pallas import tpu as pltpu
from jax.sharding import Mesh
from jax.sharding import PartitionSpec as P

NY, NZ, NX, NC = 4, 16, 4, 2
NA = NX * NC
NUB, UB, SIDE, DET = 5, 64, 256, 320
HALF = SIDE // 2
HIGHEST = lax.Precision.HIGHEST
QC = UB // NY
LANES = 2 * DET
LIMIT = 16 << 20
SLAB = ("y", "z")
ANGLE = ("x", "core")


def dft_tables():
    n, k = np.arange(HALF)[:, None], 2 * np.arange(HALF)[None, :]
    out = []
    for odd in range(2):
        ph = (n * (k + odd) % SIDE) * (2.0 * np.pi / SIDE)
        c, s = np.cos(ph) / np.sqrt(SIDE), np.sin(ph) / np.sqrt(SIDE)
        full = np.block([[c, -s], [s, c]])
        hi = full.astype(jnp.bfloat16)
        out += [hi, (full - hi.astype(np.float64)).astype(jnp.bfloat16)]
    return np.stack(out + [t.T for t in out])


def even_first():
    order = np.concatenate([np.arange(0, SIDE, 2), np.arange(1, SIDE, 2)])
    return np.eye(SIDE, dtype=np.float32)[order]


def split(v):
    hi = v.astype(jnp.bfloat16)
    return hi, (v - hi.astype(jnp.float32)).astype(jnp.bfloat16)


def dot(a, b):
    return jnp.dot(a, b, preferred_element_type=jnp.float32)


def times(v, hi, lo):
    vh, vl = split(v)
    return dot(vh, hi) + dot(vl, hi) + dot(vh, lo)


def of(hi, lo, v):
    vh, vl = split(v)
    return dot(hi, vh) + dot(hi, vl) + dot(lo, vh)


def lanes(*parts):
    return jnp.concatenate(parts, axis=1)


def rows(*parts):
    return jnp.concatenate(parts, axis=0)


def halves(v, axis):
    a, b = (v[:, :HALF], v[:, HALF:]) if axis else (v[:HALF], v[HALF:])
    return a + b, a - b


def spot_kernel(where_ref, tr_ref, ti_ref, probe_ref, power_ref, tab_ref, resid_ref, keep_ref, send_ref, grads_ref, placed_ref, far_ref, det_ref):
    even, odd, even_t, odd_t = ((tab_ref[2 * i], tab_ref[2 * i + 1]) for i in range(4))
    first = where_ref[0] == 0
    resid_ref[...] = -power_ref[...]
    for m in range(4):
        tr, ti = tr_ref[...], ti_ref[...]
        pr, pi = (probe_ref[2 * m + k].astype(jnp.float32) for k in range(2))
        sr, dr = halves(pr * tr - pi * ti, 1)
        si, di = halves(pr * ti + pi * tr, 1)
        me, mo = times(lanes(sr, si), *even), times(lanes(dr, di), *odd)
        sr, dr = halves(lanes(me[:, :HALF], mo[:, :HALF]), 0)
        si, di = halves(lanes(me[:, HALF:], mo[:, HALF:]), 0)
        fe, fo = of(*even_t, rows(sr, si)), of(*odd_t, rows(dr, di))
        far_ref[m, :SIDE] = fe
        far_ref[m, SIDE:] = fo
        resid_ref[...] += rows(fe[:HALF] * fe[:HALF] + fe[HALF:] * fe[HALF:], fo[:HALF] * fo[:HALF] + fo[HALF:] * fo[HALF:])
    grads_ref[...] = jnp.zeros_like(grads_ref)
    for m in range(4):
        tr, ti = tr_ref[...], ti_ref[...]
        pr, pi = (probe_ref[2 * m + k].astype(jnp.float32) for k in range(2))
        twice = 2.0 * resid_ref[...]
        te, to = twice[:HALF], twice[HALF:]
        be = of(*even, far_ref[m, :SIDE] * rows(te, te))
        bo = of(*odd, far_ref[m, SIDE:] * rows(to, to))
        top, bottom = be + bo, be - bo
        br, bi = rows(top[:HALF], bottom[:HALF]), rows(top[HALF:], bottom[HALF:])
        ge = times(lanes(br[:, :HALF], bi[:, :HALF]), *even_t)
        go = times(lanes(br[:, HALF:], bi[:, HALF:]), *odd_t)
        left, right = ge + go, ge - go
        gr, gi = lanes(left[:, :HALF], right[:, :HALF]), lanes(left[:, HALF:], right[:, HALF:])
        qr, qi = tr * gr + ti * gi, tr * gi - ti * gr
        keep_ref[m] = jnp.where(first, qr, qi)
        send_ref[m] = jnp.where(first, qi, qr)
        grads_ref[0] += pr * qi - pi * qr
        grads_ref[1] -= pr * qr + pi * qi
    col, row = where_ref[1], where_ref[2]
    blank = jnp.zeros((SIDE, 128), jnp.float32)
    g0 = pltpu.roll(jnp.concatenate([grads_ref[0], blank], axis=1), row, 1)
    g1 = pltpu.roll(jnp.concatenate([grads_ref[1], blank], axis=1), row + 64, 1)
    det_ref[...] = jnp.zeros_like(det_ref)
    wide = jnp.concatenate([g0[:, :256], g0[:, 256:] + g1[:, :128], g1[:, 128:]], axis=1)
    wide = jnp.concatenate([wide, jnp.zeros((8, LANES), jnp.float32)], axis=0)
    start = pl.multiple_of((col >> 3) << 3, 8)
    det_ref[pl.ds(start, SIDE + 8), :] = pltpu.roll(wide, col & 7, 0)
    for y in range(NY):
        for g in range(10):
            at = (g // 2) * UB + y * QC + (g % 2) * 8
            for t in range(5):
                placed_ref[y, g * 5 + t] = det_ref[at : at + 8, t * 128 : (t + 1) * 128]


def spot(where, tr, ti, probe, power, tab):
    f32 = jnp.float32
    plane = jax.ShapeDtypeStruct((SIDE, SIDE), f32)
    half = jax.ShapeDtypeStruct((4, SIDE, SIDE), f32)
    vmem = pl.BlockSpec(memory_space=pltpu.VMEM)
    return pl.pallas_call(
        spot_kernel,
        out_shape=(
            plane,
            half,
            half,
            jax.ShapeDtypeStruct((2, SIDE, SIDE), f32),
            jax.ShapeDtypeStruct((NY, 50, 8, 128), f32),
        ),
        in_specs=[pl.BlockSpec(memory_space=pltpu.SMEM)] + [vmem] * 5,
        out_specs=(vmem,) * 5,
        scratch_shapes=[
            pltpu.VMEM((4, 2 * SIDE, SIDE), f32),
            pltpu.VMEM((DET, LANES), f32),
        ],
        compiler_params=pltpu.CompilerParams(vmem_limit_bytes=LIMIT),
        name="spot",
    )(where, tr, ti, probe, power, tab)


def rays_kernel(vol_hbm, mat_hbm, out_ref, vol_ref, mat_ref, tile_ref, sems):
    first = pltpu.make_async_copy(vol_hbm, vol_ref, sems.at[0])
    second = pltpu.make_async_copy(mat_hbm, mat_ref, sems.at[1])
    first.start()
    second.start()
    first.wait()
    second.wait()
    tile_ref[:, :DET] = vol_ref[0].astype(jnp.float32)
    tile_ref[:, DET:] = vol_ref[1].astype(jnp.float32)
    tile = tile_ref[...].astype(jnp.bfloat16)
    for a in range(NA):
        sums = dot(mat_ref[a], tile)
        for y in range(NY):
            out_ref[y * NA + a] = sums[y * QC : (y + 1) * QC]


def rays_of(volume, matrices):
    vmem = pl.BlockSpec(memory_space=pltpu.VMEM)
    return pl.pallas_call(
        rays_kernel,
        out_shape=jax.ShapeDtypeStruct((32, QC, LANES), jnp.float32),
        in_specs=[pl.BlockSpec(memory_space=pltpu.HBM)] * 2,
        out_specs=vmem,
        scratch_shapes=[
            pltpu.VMEM((2, 128, DET), jnp.bfloat16),
            pltpu.VMEM((NA, UB, 128), jnp.bfloat16),
            pltpu.VMEM((128, LANES), jnp.float32),
            pltpu.SemaphoreType.DMA((2,)),
        ],
        name="rays",
    )(volume, matrices)


def volume_kernel(y_ref, got_ref, mat_ref, vol_ref, probe_ref, hi_ref, lo_ref):
    for a in range(NA):
        for y in range(NY):
            at = a * UB + y * QC
            for t in range(5):
                v = jnp.concatenate([got_ref[y * NA + a, t], got_ref[y * NA + a, 5 + t]], axis=0)
                hi, lo = split(v)
                hi_ref[at : at + QC, t * 128 : (t + 1) * 128] = hi
                lo_ref[at : at + QC, t * 128 : (t + 1) * 128] = lo
    back = lambda ref: lax.dot_general(
        mat_ref[...], ref[...], (((0,), (0,)), ((), ())), preferred_element_type=jnp.float32
    )
    grad = back(hi_ref) + back(lo_ref)
    vol_ref[0] = grad[:, :DET]
    vol_ref[1] = pltpu.roll(grad, DET, 1)[:, :DET]
    for a in range(NA):
        piece = got_ref[y_ref[0] * NA + a, 10]
        for r in range(4):
            for k in range(2):
                probe_ref[a, r : r + 1, k * 128 : (k + 1) * 128] = piece[2 * r + k : 2 * r + k + 1]


def volume_of(y, got, matrices):
    vmem = pl.BlockSpec(memory_space=pltpu.VMEM)
    return pl.pallas_call(
        volume_kernel,
        out_shape=(
            jax.ShapeDtypeStruct((2, 128, DET), jnp.float32),
            jax.ShapeDtypeStruct((NA, 4, SIDE), jnp.float32),
        ),
        in_specs=[pl.BlockSpec(memory_space=pltpu.SMEM)] + [vmem] * 2,
        out_specs=(vmem,) * 2,
        scratch_shapes=[pltpu.VMEM((512, LANES), jnp.bfloat16)] * 2,
        compiler_params=pltpu.CompilerParams(vmem_limit_bytes=LIMIT),
        name="volume",
    )(y, got, matrices)


def blocks_kernel(ids_ref, quarter_ref, piece_ref, out_ref):
    for i in range(32):
        at = ids_ref[i] * 10
        for v in range(10):
            out_ref[i, v] = quarter_ref[at + v]
        out_ref[i, 10] = piece_ref[...]


def blocks_of(ids, quarter, piece):
    vmem = pl.BlockSpec(memory_space=pltpu.VMEM)
    return pl.pallas_call(
        blocks_kernel,
        out_shape=jax.ShapeDtypeStruct((32, 11, 8, 128), jnp.float32),
        in_specs=[pl.BlockSpec(memory_space=pltpu.SMEM)] + [vmem] * 2,
        out_specs=vmem,
        compiler_params=pltpu.CompilerParams(vmem_limit_bytes=LIMIT),
        name="blocks",
    )(ids, quarter, piece)


def exchange(x, axes):
    return lax.all_to_all(x, axes, split_axis=0, concat_axis=0, tiled=True)


def to_tiles(q):
    n = q.shape[0] // 8
    return q.reshape(n, 8, 5, 128).transpose(0, 2, 1, 3).reshape(n * 5, 8, 128)


def from_tiles(t):
    n = t.shape[0] // 5
    return t.reshape(n, 5, 8, 128).transpose(0, 2, 1, 3).reshape(n * 8, LANES)


def chunks_of_z(tiles):
    return tiles.reshape(NZ, 25, 1, 128)


def pick(x, i, n):
    return lax.dynamic_index_in_dim(x, i % n, 0, keepdims=False)


def shift(x, axis, size, by):
    return lax.ppermute(x, axis, [(i, (i + by) % size) for i in range(size)])


def step(volume, matrices, tile_ids, modes, corners, power):
    y, z = lax.axis_index("y"), lax.axis_index("z")
    angle = lax.axis_index(ANGLE)
    ids = lax.dynamic_index_in_dim(tile_ids, angle, 0, keepdims=False)
    ids = lax.dynamic_index_in_dim(ids.reshape(NY, NZ, NA), z, 1, keepdims=False).reshape(32)

    items = exchange(rays_of(volume.reshape(2, 128, DET), matrices), ("y", "x", "core"))
    quarter = jnp.stack(
        [jnp.sum(jnp.where((ids == d)[:, None, None], items, 0.0), axis=0) for d in range(NUB)]
    )
    mine = exchange(chunks_of_z(to_tiles(quarter.reshape(NUB * QC, LANES))), "z").sum(0)
    copies = jnp.broadcast_to(mine[None], (NZ, 25, 1, 128))
    summed = exchange(copies, "z").reshape(50, 8, 128)
    every = lax.all_gather(summed, "y", axis=0, tiled=False)
    det = from_tiles(every.reshape(200, 8, 128))
    det = det.reshape(NY, NUB, QC, LANES).transpose(1, 0, 2, 3).reshape(DET, LANES)

    col, row = corners[0, 0, 0], corners[0, 0, 1]
    wins = [lax.dynamic_slice(det, (col - 1, k * DET + row - 1), (SIDE + 2, SIDE + 2)) for k in range(2)]
    p0, p1 = wins[0][1:-1, 1:-1], wins[1][1:-1, 1:-1]
    absorb = jnp.exp(-p1)
    tr, ti = absorb * jnp.cos(p0), absorb * jnp.sin(p0)
    core = lax.axis_index("core")
    order = jnp.asarray(even_first())
    turn = lambda p, v: jnp.dot(jnp.dot(p, v, precision=HIGHEST), p.T, precision=HIGHEST)
    resid, keep, send, grads, placed = spot(
        jnp.stack([core, col, row]), tr, ti, modes.reshape(8, SIDE, SIDE), turn(order, power[0, 0]), jnp.asarray(dft_tables())
    )
    resid = turn(order.T, resid)

    d_col = sum(jnp.sum(g_ * (w[2:, 1:-1] - w[:-2, 1:-1])) for g_, w in zip((grads[0], grads[1]), wins))
    d_row = sum(jnp.sum(g_ * (w[1:-1, 2:] - w[1:-1, :-2])) for g_, w in zip((grads[0], grads[1]), wins))
    locus = (jnp.stack([d_col, d_row]) * (0.5 / SIDE))[None, None]

    other = shift(send, "core", NC, 1)
    planes = keep + other
    got = [shift(pick(planes, lax.axis_index("x") + k, NX), "x", NX, k) for k in (2, 1, 3)]
    rows = (pick(planes, lax.axis_index("x"), NX) + got[0] + got[1] + got[2]).reshape(NY, 64, SIDE)
    got = [shift(pick(rows, y + k, NY), "y", NY, k) for k in (2, 1, 3)]
    rows = (pick(rows, y, NY) + got[0] + got[1] + got[2]).reshape(NZ, 8, 1, 128)

    part = exchange(placed, "y")
    part = part.sum(0)
    part = exchange(chunks_of_z(part), "z")
    mine = part.sum(0)
    got = exchange(jnp.concatenate([jnp.broadcast_to(mine[None], (NZ, 25, 1, 128)), rows], axis=1), "z")
    piece = got[:, 25:].sum(0).reshape(8, 128)
    sent = blocks_of(ids, got[:, :25].reshape(50, 8, 128), piece)
    got = exchange(sent, ("y", "x", "core"))
    vol_grad, probe_grad = volume_of(y.reshape(1), got, matrices.reshape(512, 128))
    vol_grad = vol_grad.reshape(2, 8, 16, DET)
    probe_grad = probe_grad.reshape(4, 2, 4, SIDE)
    return vol_grad, probe_grad, resid[None, None], locus


def solution(mesh):
    mesh = Mesh(mesh.devices.reshape(NY, NZ, NX, NC), ("y", "z", "x", "core"))
    in_specs = (
        P(None, SLAB, ANGLE, None),
        P(),
        P(),
        P(),
        P(ANGLE, SLAB, None),
        P(ANGLE, SLAB, None, None),
    )
    out_specs = (
        P(None, SLAB, ANGLE, None),
        P(None, None, SLAB, None),
        P(ANGLE, SLAB, None, None),
        P(ANGLE, SLAB, None),
    )
    return jax.shard_map(step, mesh=mesh, in_specs=in_specs, out_specs=out_specs, check_vma=False)
```

```python
import numpy as np

import jax
import jax.numpy as jnp
from jax import lax
from jax.experimental import pallas as pl
from jax.experimental.pallas import tpu as pltpu
from jax.sharding import Mesh
from jax.sharding import PartitionSpec as P

NY, NZ, NX, NC = 4, 16, 4, 2
NA = NX * NC
NUB, UB, SIDE, DET = 5, 64, 256, 320
HALF = SIDE // 2
HIGHEST = lax.Precision.HIGHEST
QC = UB // NY
LANES = 2 * DET
LIMIT = 16 << 20
SLAB = ("y", "z")
ANGLE = ("x", "core")


def dft_tables():
    n, k = np.arange(HALF)[:, None], 2 * np.arange(HALF)[None, :]
    out = []
    for odd in range(2):
        ph = (n * (k + odd) % SIDE) * (2.0 * np.pi / SIDE)
        c, s = np.cos(ph) / np.sqrt(SIDE), np.sin(ph) / np.sqrt(SIDE)
        full = np.block([[c, -s], [s, c]])
        hi = full.astype(jnp.bfloat16)
        out += [hi, (full - hi.astype(np.float64)).astype(jnp.bfloat16)]
    return np.stack(out + [t.T for t in out])


def even_first():
    order = np.concatenate([np.arange(0, SIDE, 2), np.arange(1, SIDE, 2)])
    return np.eye(SIDE, dtype=np.float32)[order]


def split(v):
    hi = v.astype(jnp.bfloat16)
    return hi, (v - hi.astype(jnp.float32)).astype(jnp.bfloat16)


def dot(a, b):
    return jnp.dot(a, b, preferred_element_type=jnp.float32)


def times(v, hi, lo):
    vh, vl = split(v)
    return dot(vh, hi) + dot(vl, hi) + dot(vh, lo)


def of(hi, lo, v):
    vh, vl = split(v)
    return dot(hi, vh) + dot(hi, vl) + dot(lo, vh)


def lanes(*parts):
    return jnp.concatenate(parts, axis=1)


def rows(*parts):
    return jnp.concatenate(parts, axis=0)


def halves(v, axis):
    a, b = (v[:, :HALF], v[:, HALF:]) if axis else (v[:HALF], v[HALF:])
    return a + b, a - b


def spot_kernel(where_ref, tr_ref, ti_ref, probe_ref, power_ref, tab_ref, resid_ref, keep_ref, send_ref, grads_ref, placed_ref, far_ref, det_ref):
    even, odd, even_t, odd_t = ((tab_ref[2 * i], tab_ref[2 * i + 1]) for i in range(4))
    first = where_ref[0] == 0
    resid_ref[...] = -power_ref[...]
    for m in range(4):
        tr, ti = tr_ref[...], ti_ref[...]
        pr, pi = (probe_ref[2 * m + k].astype(jnp.float32) for k in range(2))
        sr, dr = halves(pr * tr - pi * ti, 1)
        si, di = halves(pr * ti + pi * tr, 1)
        me, mo = times(lanes(sr, si), *even), times(lanes(dr, di), *odd)
        sr, dr = halves(lanes(me[:, :HALF], mo[:, :HALF]), 0)
        si, di = halves(lanes(me[:, HALF:], mo[:, HALF:]), 0)
        fe, fo = of(*even_t, rows(sr, si)), of(*odd_t, rows(dr, di))
        far_ref[m, :SIDE] = fe
        far_ref[m, SIDE:] = fo
        resid_ref[...] += rows(fe[:HALF] * fe[:HALF] + fe[HALF:] * fe[HALF:], fo[:HALF] * fo[:HALF] + fo[HALF:] * fo[HALF:])
    grads_ref[...] = jnp.zeros_like(grads_ref)
    for m in range(4):
        tr, ti = tr_ref[...], ti_ref[...]
        pr, pi = (probe_ref[2 * m + k].astype(jnp.float32) for k in range(2))
        twice = 2.0 * resid_ref[...]
        te, to = twice[:HALF], twice[HALF:]
        be = of(*even, far_ref[m, :SIDE] * rows(te, te))
        bo = of(*odd, far_ref[m, SIDE:] * rows(to, to))
        top, bottom = be + bo, be - bo
        br, bi = rows(top[:HALF], bottom[:HALF]), rows(top[HALF:], bottom[HALF:])
        ge = times(lanes(br[:, :HALF], bi[:, :HALF]), *even_t)
        go = times(lanes(br[:, HALF:], bi[:, HALF:]), *odd_t)
        left, right = ge + go, ge - go
        gr, gi = lanes(left[:, :HALF], right[:, :HALF]), lanes(left[:, HALF:], right[:, HALF:])
        qr, qi = tr * gr + ti * gi, tr * gi - ti * gr
        keep_ref[m] = jnp.where(first, qr, qi)
        send_ref[m] = jnp.where(first, qi, qr)
        grads_ref[0] += pr * qi - pi * qr
        grads_ref[1] -= pr * qr + pi * qi
    col, row = where_ref[1], where_ref[2]
    blank = jnp.zeros((SIDE, 128), jnp.float32)
    g0 = pltpu.roll(jnp.concatenate([grads_ref[0], blank], axis=1), row, 1)
    g1 = pltpu.roll(jnp.concatenate([grads_ref[1], blank], axis=1), row + 64, 1)
    det_ref[...] = jnp.zeros_like(det_ref)
    wide = jnp.concatenate([g0[:, :256], g0[:, 256:] + g1[:, :128], g1[:, 128:]], axis=1)
    wide = jnp.concatenate([wide, jnp.zeros((8, LANES), jnp.float32)], axis=0)
    start = pl.multiple_of((col >> 3) << 3, 8)
    det_ref[pl.ds(start, SIDE + 8), :] = pltpu.roll(wide, col & 7, 0)
    for y in range(NY):
        for g in range(10):
            at = (g // 2) * UB + y * QC + (g % 2) * 8
            for t in range(5):
                placed_ref[y, g * 5 + t] = det_ref[at : at + 8, t * 128 : (t + 1) * 128]


def spot(where, tr, ti, probe, power, tab):
    f32 = jnp.float32
    plane = jax.ShapeDtypeStruct((SIDE, SIDE), f32)
    half = jax.ShapeDtypeStruct((4, SIDE, SIDE), f32)
    vmem = pl.BlockSpec(memory_space=pltpu.VMEM)
    return pl.pallas_call(
        spot_kernel,
        out_shape=(
            plane,
            half,
            half,
            jax.ShapeDtypeStruct((2, SIDE, SIDE), f32),
            jax.ShapeDtypeStruct((NY, 50, 8, 128), f32),
        ),
        in_specs=[pl.BlockSpec(memory_space=pltpu.SMEM)] + [vmem] * 5,
        out_specs=(vmem,) * 5,
        scratch_shapes=[
            pltpu.VMEM((4, 2 * SIDE, SIDE), f32),
            pltpu.VMEM((DET, LANES), f32),
        ],
        compiler_params=pltpu.CompilerParams(vmem_limit_bytes=LIMIT),
        name="spot",
    )(where, tr, ti, probe, power, tab)


def rays_kernel(vol_hbm, mat_hbm, out_ref, vol_ref, mat_ref, tile_ref, sems):
    first = pltpu.make_async_copy(vol_hbm, vol_ref, sems.at[0])
    second = pltpu.make_async_copy(mat_hbm, mat_ref, sems.at[1])
    first.start()
    second.start()
    first.wait()
    second.wait()
    tile_ref[:, :DET] = vol_ref[0].astype(jnp.float32)
    tile_ref[:, DET:] = vol_ref[1].astype(jnp.float32)
    tile = tile_ref[...].astype(jnp.bfloat16)
    for a in range(NA):
        sums = dot(mat_ref[a], tile)
        for y in range(NY):
            out_ref[y * NA + a] = sums[y * QC : (y + 1) * QC]


def rays_of(volume, matrices):
    vmem = pl.BlockSpec(memory_space=pltpu.VMEM)
    return pl.pallas_call(
        rays_kernel,
        out_shape=jax.ShapeDtypeStruct((32, QC, LANES), jnp.float32),
        in_specs=[pl.BlockSpec(memory_space=pltpu.HBM)] * 2,
        out_specs=vmem,
        scratch_shapes=[
            pltpu.VMEM((2, 128, DET), jnp.bfloat16),
            pltpu.VMEM((NA, UB, 128), jnp.bfloat16),
            pltpu.VMEM((128, LANES), jnp.float32),
            pltpu.SemaphoreType.DMA((2,)),
        ],
        name="rays",
    )(volume, matrices)


def volume_kernel(y_ref, got_ref, mat_ref, vol_ref, probe_ref, hi_ref, lo_ref):
    for a in range(NA):
        for y in range(NY):
            at = a * UB + y * QC
            for t in range(5):
                v = jnp.concatenate([got_ref[y * NA + a, t], got_ref[y * NA + a, 5 + t]], axis=0)
                hi, lo = split(v)
                hi_ref[at : at + QC, t * 128 : (t + 1) * 128] = hi
                lo_ref[at : at + QC, t * 128 : (t + 1) * 128] = lo
    back = lambda ref: lax.dot_general(
        mat_ref[...], ref[...], (((0,), (0,)), ((), ())), preferred_element_type=jnp.float32
    )
    grad = back(hi_ref) + back(lo_ref)
    vol_ref[0] = grad[:, :DET]
    vol_ref[1] = pltpu.roll(grad, DET, 1)[:, :DET]
    for a in range(NA):
        piece = got_ref[y_ref[0] * NA + a, 10]
        for r in range(4):
            for k in range(2):
                probe_ref[a, r : r + 1, k * 128 : (k + 1) * 128] = piece[2 * r + k : 2 * r + k + 1]


def volume_of(y, got, matrices):
    vmem = pl.BlockSpec(memory_space=pltpu.VMEM)
    return pl.pallas_call(
        volume_kernel,
        out_shape=(
            jax.ShapeDtypeStruct((2, 128, DET), jnp.float32),
            jax.ShapeDtypeStruct((NA, 4, SIDE), jnp.float32),
        ),
        in_specs=[pl.BlockSpec(memory_space=pltpu.SMEM)] + [vmem] * 2,
        out_specs=(vmem,) * 2,
        scratch_shapes=[pltpu.VMEM((512, LANES), jnp.bfloat16)] * 2,
        compiler_params=pltpu.CompilerParams(vmem_limit_bytes=LIMIT),
        name="volume",
    )(y, got, matrices)


def blocks_kernel(ids_ref, quarter_ref, piece_ref, out_ref):
    for i in range(32):
        at = ids_ref[i] * 10
        for v in range(10):
            out_ref[i, v] = quarter_ref[at + v]
        out_ref[i, 10] = piece_ref[...]


def blocks_of(ids, quarter, piece):
    vmem = pl.BlockSpec(memory_space=pltpu.VMEM)
    return pl.pallas_call(
        blocks_kernel,
        out_shape=jax.ShapeDtypeStruct((32, 11, 8, 128), jnp.float32),
        in_specs=[pl.BlockSpec(memory_space=pltpu.SMEM)] + [vmem] * 2,
        out_specs=vmem,
        compiler_params=pltpu.CompilerParams(vmem_limit_bytes=LIMIT),
        name="blocks",
    )(ids, quarter, piece)


def add_kernel(parts_ref, out_ref):
    out_ref[...] = (parts_ref[0] + parts_ref[1]) + (parts_ref[2] + parts_ref[3])


def add_shares(parts):
    vmem = pl.BlockSpec(memory_space=pltpu.VMEM)
    return pl.pallas_call(
        add_kernel,
        out_shape=jax.ShapeDtypeStruct((50, 8, 128), jnp.float32),
        in_specs=[vmem],
        out_specs=vmem,
        compiler_params=pltpu.CompilerParams(vmem_limit_bytes=LIMIT),
        name="add",
    )(parts)


def exchange(x, axes):
    return lax.all_to_all(x, axes, split_axis=0, concat_axis=0, tiled=True)


def to_tiles(q):
    n = q.shape[0] // 8
    return q.reshape(n, 8, 5, 128).transpose(0, 2, 1, 3).reshape(n * 5, 8, 128)


def from_tiles(t):
    n = t.shape[0] // 5
    return t.reshape(n, 5, 8, 128).transpose(0, 2, 1, 3).reshape(n * 8, LANES)


def chunks_of_z(tiles):
    return tiles.reshape(NZ, 25, 1, 128)


def pick(x, i, n):
    return lax.dynamic_index_in_dim(x, i % n, 0, keepdims=False)


def shift(x, axis, size, by):
    return lax.ppermute(x, axis, [(i, (i + by) % size) for i in range(size)])


def step(volume, matrices, tile_ids, modes, corners, power):
    y, z = lax.axis_index("y"), lax.axis_index("z")
    angle = lax.axis_index(ANGLE)
    ids = lax.dynamic_index_in_dim(tile_ids, angle, 0, keepdims=False)
    ids = lax.dynamic_index_in_dim(ids.reshape(NY, NZ, NA), z, 1, keepdims=False).reshape(32)

    items = exchange(rays_of(volume.reshape(2, 128, DET), matrices), ("y", "x", "core"))
    quarter = jnp.stack(
        [jnp.sum(jnp.where((ids == d)[:, None, None], items, 0.0), axis=0) for d in range(NUB)]
    )
    mine = exchange(chunks_of_z(to_tiles(quarter.reshape(NUB * QC, LANES))), "z").sum(0)
    copies = jnp.broadcast_to(mine[None], (NZ, 25, 1, 128))
    summed = exchange(copies, "z").reshape(50, 8, 128)
    every = lax.all_gather(summed, "y", axis=0, tiled=False)
    det = from_tiles(every.reshape(200, 8, 128))
    det = det.reshape(NY, NUB, QC, LANES).transpose(1, 0, 2, 3).reshape(DET, LANES)

    col, row = corners[0, 0, 0], corners[0, 0, 1]
    wins = [lax.dynamic_slice(det, (col - 1, k * DET + row - 1), (SIDE + 2, SIDE + 2)) for k in range(2)]
    p0, p1 = wins[0][1:-1, 1:-1], wins[1][1:-1, 1:-1]
    absorb = jnp.exp(-p1)
    tr, ti = absorb * jnp.cos(p0), absorb * jnp.sin(p0)
    core = lax.axis_index("core")
    order = jnp.asarray(even_first())
    turn = lambda p, v: jnp.dot(jnp.dot(p, v, precision=HIGHEST), p.T, precision=HIGHEST)
    resid, keep, send, grads, placed = spot(
        jnp.stack([core, col, row]), tr, ti, modes.reshape(8, SIDE, SIDE), turn(order, power[0, 0]), jnp.asarray(dft_tables())
    )
    resid = turn(order.T, resid)

    d_col = sum(jnp.sum(g_ * (w[2:, 1:-1] - w[:-2, 1:-1])) for g_, w in zip((grads[0], grads[1]), wins))
    d_row = sum(jnp.sum(g_ * (w[1:-1, 2:] - w[1:-1, :-2])) for g_, w in zip((grads[0], grads[1]), wins))
    locus = (jnp.stack([d_col, d_row]) * (0.5 / SIDE))[None, None]

    other = shift(send, "core", NC, 1)
    planes = keep + other
    got = [shift(pick(planes, lax.axis_index("x") + k, NX), "x", NX, k) for k in (2, 1, 3)]
    rows = (pick(planes, lax.axis_index("x"), NX) + got[0] + got[1] + got[2]).reshape(NY, 64, SIDE)
    got = [shift(pick(rows, y + k, NY), "y", NY, k) for k in (2, 1, 3)]
    rows = (pick(rows, y, NY) + got[0] + got[1] + got[2]).reshape(NZ, 8, 1, 128)

    part = exchange(placed, "y")
    part = add_shares(part)
    part = exchange(chunks_of_z(part), "z")
    mine = part.sum(0)
    got = exchange(jnp.concatenate([jnp.broadcast_to(mine[None], (NZ, 25, 1, 128)), rows], axis=1), "z")
    piece = got[:, 25:].sum(0).reshape(8, 128)
    sent = blocks_of(ids, got[:, :25].reshape(50, 8, 128), piece)
    got = exchange(sent, ("y", "x", "core"))
    vol_grad, probe_grad = volume_of(y.reshape(1), got, matrices.reshape(512, 128))
    vol_grad = vol_grad.reshape(2, 8, 16, DET)
    probe_grad = probe_grad.reshape(4, 2, 4, SIDE)
    return vol_grad, probe_grad, resid[None, None], locus


def solution(mesh):
    mesh = Mesh(mesh.devices.reshape(NY, NZ, NX, NC), ("y", "z", "x", "core"))
    in_specs = (
        P(None, SLAB, ANGLE, None),
        P(),
        P(),
        P(),
        P(ANGLE, SLAB, None),
        P(ANGLE, SLAB, None, None),
    )
    out_specs = (
        P(None, SLAB, ANGLE, None),
        P(None, None, SLAB, None),
        P(ANGLE, SLAB, None, None),
        P(ANGLE, SLAB, None),
    )
    return jax.shard_map(step, mesh=mesh, in_specs=in_specs, out_specs=out_specs, check_vma=False)
```
